512 devices in a mesh: row: 32 (over z_hi, x, core), col: 16 (over z_lo, y).
Axes of the slice: x: 4, y: 4, z: 16 (z_hi: 4, z_lo: 4; z = z_hi * 4 + z_lo), core: 2. Of those that a mesh axis runs over, the one named last changes fastest.
Arguments:
- positions: float32 [3, 262144], P(None, ('row', 'col')), may hold values from 0 to 170
- velocities: float32 [3, 262144], P(None, ('row', 'col')), may hold values from -6 to 6
- old_forces: float32 [3, 262144], P(None, ('row', 'col')), may hold values from -40 to 40
- types: int32 [262144], P(('row', 'col')), may hold values from 0 to 17
- sigma_table: float32 [18], replicated, may hold values from 0.8 to 1.2
- epsilon_table: float32 [18], replicated, may hold values from 0.1 to 1
- pairs: int32 [32, 16, 2, 128], P('row', 'col'), may hold values from 0 to 127, as said below
- live: int32 [32, 16], P('row', 'col'), may hold values from 56 to 128
Outputs:
- moved: float32 [3, 262144], P(None, ('row', 'col'))
- new_velocities: float32 [3, 262144], P(None, ('row', 'col'))
- new_forces: float32 [3, 262144], P(None, ('row', 'col'))
The draws below stay inside these ranges and needn't reach their ends.
Inputs may be any that keep to these rules, and one draw needn't show every extreme that they name: pairs[r, c, 0, p] is below 64 and pairs[r, c, 1, p] below 128; the slots of one cell name distinct ordered block pairs.
All inputs are finite; a program needn't handle non-finite values.
Results may differ from the reference program's by a relative error of at most 0.0003.
Values sent between devices are 32-bit elements; how exact they have to be, the bound alone decides.
A program may use at most 64 MiB of HBM per device.

```python
import math
import jax
import jax.numpy as jnp
import numpy as np
from jax import lax

BLK = 128
BPD = 4
P_DEV = 128
NT = 18
GRID_R = 32
GRID_C = 16
N_BEAD = 262144


cell_side = 5.3


def offset_table():
    listed = []
    for step_y in (-1, 0, 1):
        for step_z in (-1, 0, 1):
            listed.append((1, step_y, step_z))
    for step_z in (-1, 0, 1):
        listed.append((0, 1, step_z))
    listed.append((0, 0, 1))
    listed.append((0, 0, 0))
    for step_y in (-1, 0, 1):
        for step_z in (-1, 0, 1):
            listed.append((2, step_y, step_z))
    for step_x in (-1, 0, 1):
        for step_z in (-1, 0, 1):
            listed.append((step_x, 2, step_z))
    return np.array(listed, dtype=np.int32)


def lattice_shifts(key):
    base = jax.random.fold_in(key, 101)
    row_shift = jax.random.randint(jax.random.fold_in(base, 1), (BPD,), 0, GRID_R)
    col_shift = jax.random.randint(jax.random.fold_in(base, 2), (BPD,), 0, GRID_C)
    places = jnp.arange(BPD)
    row_half = (row_shift[0] + GRID_R // 2) % GRID_R
    col_half = (col_shift[0] + GRID_C // 2) % GRID_C
    row_shift = jnp.where(places == 1, row_half, row_shift)
    col_shift = jnp.where(places == 1, col_half, col_shift)
    row_shift = jnp.where(places == 2, (row_half + 1) % GRID_R, row_shift)
    col_shift = jnp.where(places == 2, (col_half + 1) % GRID_C, col_shift)
    return (row_shift.astype(jnp.int32), col_shift.astype(jnp.int32))


def skin_counts(key):
    cells = GRID_R * GRID_C
    room = 18 * BPD
    base = jax.random.fold_in(key, 202)
    tries = jax.random.randint(jax.random.fold_in(base, 1), (3, cells), 0, room + 1)
    counts = jnp.min(tries, axis=0)
    fullest = jax.random.randint(jax.random.fold_in(base, 2), (), 0, cells)
    emptiest = (fullest + 1 + jax.random.randint(jax.random.fold_in(base, 3), (), 0, cells - 1)) % cells
    places = jnp.arange(cells)
    counts = jnp.where(places == fullest, room, counts)
    counts = jnp.where(places == emptiest, 0, counts)
    return counts.astype(jnp.int32)


def draw_positions(key, part):
    row_shift, col_shift = lattice_shifts(key)
    blocks = jnp.arange(N_BEAD // BLK, dtype=jnp.int32)
    layer = blocks % BPD
    shard = blocks // BPD
    along_y = (shard // GRID_C + row_shift[layer]) % GRID_R
    along_z = (shard % GRID_C + col_shift[layer]) % GRID_C
    corner = jnp.stack([layer, along_y, along_z]).astype(jnp.float32)
    corner = jnp.repeat(corner, BLK, axis=1)
    inside = jax.random.uniform(jax.random.fold_in(key, 7), (3, N_BEAD), jnp.float32)
    return (corner + inside) * cell_side


def draw_pairs(key, part):
    row_shift, col_shift = lattice_shifts(key)
    counts = skin_counts(key)
    table = offset_table()
    kinds = table.shape[0]
    total = BPD * kinds
    cells = GRID_R * GRID_C
    along_x = jnp.asarray(table[:, 0])[None, :]
    along_y = jnp.asarray(table[:, 1])[None, :]
    along_z = jnp.asarray(table[:, 2])[None, :]
    layer = jnp.arange(BPD, dtype=jnp.int32)[:, None]
    partner = (layer + along_x) % BPD
    col_step = (col_shift[partner] - along_z - col_shift[layer]) % GRID_C
    row_step = (row_shift[layer] + along_y - row_shift[partner]) % GRID_R
    row_ids = jnp.arange(GRID_R, dtype=jnp.int32)[:, None, None, None]
    col_ids = jnp.arange(GRID_C, dtype=jnp.int32)[None, :, None, None]
    local_row = (col_ids + col_step[None, None]) % GRID_C * BPD + layer[None, None]
    local_col = (row_ids + row_step[None, None]) % GRID_R * BPD + partner[None, None]
    local_row = jnp.broadcast_to(local_row, (GRID_R, GRID_C, BPD, kinds)).reshape(cells, total)
    local_col = jnp.broadcast_to(local_col, (GRID_R, GRID_C, BPD, kinds)).reshape(cells, total)
    nearby = np.tile(np.arange(kinds) < 14, BPD)
    shell_rank = (np.cumsum(~nearby) - 1).astype(np.int32)
    chosen = jnp.asarray(nearby)[None, :] | (jnp.asarray(shell_rank)[None, :] < counts[:, None])
    noise = jax.random.randint(jax.random.fold_in(key, 303), (cells, total), 0, 2 ** 20)
    index = jnp.arange(total, dtype=jnp.int32)[None, :]
    scores = jnp.where(chosen, noise, 2 ** 20 + jnp.asarray(shell_rank)[None, :]) * total + index
    order = jnp.argsort(scores, axis=1)
    local_row = jnp.take_along_axis(local_row, order, axis=1)
    local_col = jnp.take_along_axis(local_col, order, axis=1)
    joined = jnp.stack([local_row, local_col], axis=1)
    return joined.reshape(GRID_R, GRID_C, 2, total).astype(jnp.int32)


def draw_live(key, part):
    counts = skin_counts(key)
    return (14 * BPD + counts).reshape(GRID_R, GRID_C).astype(jnp.int32)


def touch_ends(values, stream_key, least, largest):
    spot = [jax.random.randint(jax.random.fold_in(stream_key, axis), (), 0, length) for axis, length in enumerate(values.shape)]
    longest = values.shape.index(max(values.shape))
    beside = spot[:longest] + [(spot[longest] + 1) % values.shape[longest]] + spot[longest + 1:]
    return values.at[tuple(spot)].set(least).at[tuple(beside)].set(largest)


def steps_of(own_key, dims, split, least, top_value):
    factor_of, own = 1.0, jax.random.fold_in(own_key, 6)
    for axis_at, blocks in split:
        heights = jnp.exp(jax.random.uniform(jax.random.fold_in(own, axis_at), (blocks,), jnp.float32, least / len(split), top_value / len(split)))
        factor_of = factor_of * jnp.repeat(heights, dims[axis_at] // blocks).reshape([-1 if axis == axis_at else 1 for axis in range(len(dims))])
    return factor_of


def bell_draw(rng, shape, width, reach, shards=(), held_as=jnp.bfloat16):
    gain = steps_of(rng, shape, shards, -0.22, 0.18) if shards else 1.0
    values = jax.random.normal(rng, shape, jnp.float32) * width * gain
    return jnp.minimum(jnp.maximum(values, -reach), reach).astype(held_as)


def setup_inputs(seed: int = 0) -> dict:
    seeds = jax.random.split(jax.random.key(seed), 9)
    return {
        "positions": draw_positions(jax.random.fold_in(seeds[8], 71), 0),
        "velocities": bell_draw(seeds[1], (3, N_BEAD), 1.0, 6.0, ((1, 512),), jnp.float32),
        "old_forces": bell_draw(seeds[2], (3, N_BEAD), 5.0, 40.0, ((1, 512),), jnp.float32),
        "types": touch_ends(jax.random.randint(seeds[3], (N_BEAD,), 0, NT), jax.random.fold_in(seeds[3], 1), 0, NT - 1).astype(jnp.int32),
        "sigma_table": jnp.clip(jax.random.uniform(seeds[4], (NT,), jnp.float32, 0.8, 1.2), 0.8, 1.2),
        "epsilon_table": jnp.clip(jnp.exp(jax.random.uniform(seeds[5], (NT,), jnp.float32, math.log(0.1), math.log(1.0))), 0.1, 1.0),
        "pairs": draw_pairs(jax.random.fold_in(seeds[8], 71), 0),
        "live": draw_live(jax.random.fold_in(seeds[8], 71), 0),
    }


time_step = 0.05
cell_side = 5.3
cutoff_sq = 6.25

def pair_terms(row_block, col_block, same, box_len):
    delta = col_block[:3, None, :] - row_block[:3, :, None]
    delta = delta - box_len * jnp.floor(delta / box_len + 0.5)
    radius_sq = lax.optimization_barrier(jnp.sum(delta * delta, axis=0))
    sig = 0.5 * (row_block[3][:, None] + col_block[3][None, :])
    depth = row_block[4][:, None] * col_block[4][None, :]
    soft_sq = radius_sq + sig * sig
    cube = (sig * sig / soft_sq) ** 3
    energy = 4.0 * depth * (cube * cube - cube)
    slope = 4.0 * depth * (2.0 * cube - 1.0) * (-3.0 * cube / soft_sq)
    weight = 1.0 - radius_sq / cutoff_sq
    coeff = 2.0 * (slope * weight * weight + energy * (-2.0 * weight / cutoff_sq))
    count = row_block.shape[1]
    upper = (jnp.arange(count)[:, None] < jnp.arange(count)[None, :]).astype(jnp.float32)
    keeper = jnp.where(same, upper, jnp.ones_like(upper))
    coeff = jnp.where(radius_sq < cutoff_sq, coeff, 0.0) * keeper
    on_row = lax.optimization_barrier(jnp.sum(coeff[None] * delta, axis=2))
    on_col = -lax.optimization_barrier(jnp.sum(coeff[None] * delta, axis=1))
    return (on_row, on_col)

def reference(positions, velocities, old_forces, types, sigma_table, epsilon_table, pairs, live):
    moved = positions + time_step * velocities + 0.5 * time_step * time_step * old_forces
    box_len = jnp.array([BPD * cell_side, GRID_R * cell_side, GRID_C * cell_side], dtype=jnp.float32)[:, None, None]
    packet = jnp.concatenate([moved, sigma_table[types][None, :], jnp.sqrt(epsilon_table)[types][None, :]], axis=0)
    row_index = jnp.arange(GRID_R, dtype=jnp.int32)[:, None, None]
    col_index = jnp.arange(GRID_C, dtype=jnp.int32)[None, :, None]
    first = row_index * (GRID_C * BPD) + pairs[:, :, 0, :]
    second_b = pairs[:, :, 1, :]
    second = (second_b // BPD * GRID_C + col_index) * BPD + second_b % BPD
    active = (jnp.arange(P_DEV, dtype=jnp.int32)[None, None, :] < live[:, :, None]).astype(jnp.float32)
    first = first.reshape(-1).astype(jnp.int32)
    second = second.reshape(-1).astype(jnp.int32)
    active = active.reshape(-1)

    def step(forces, item):
        block_x, block_y, flag = item
        row_block = lax.dynamic_slice_in_dim(packet, block_x * BLK, BLK, 1)
        col_block = lax.dynamic_slice_in_dim(packet, block_y * BLK, BLK, 1)
        on_row, on_col = pair_terms(row_block, col_block, block_x == block_y, box_len)
        old_row = lax.dynamic_slice_in_dim(forces, block_x * BLK, BLK, 1)
        forces = lax.dynamic_update_slice_in_dim(forces, old_row + flag * on_row, block_x * BLK, 1)
        old_col = lax.dynamic_slice_in_dim(forces, block_y * BLK, BLK, 1)
        forces = lax.dynamic_update_slice_in_dim(forces, old_col + flag * on_col, block_y * BLK, 1)
        return (forces, None)
    new_forces, _ = lax.scan(step, jnp.zeros((3, N_BEAD), jnp.float32), (first, second, active))
    new_velocities = velocities + 0.5 * time_step * (old_forces + new_forces)
    return (moved, new_velocities, new_forces)
```

```python
import math

import jax
import jax.numpy as jnp
from jax import lax
from jax.experimental import pallas as pl
from jax.experimental.pallas import tpu as pltpu
from jax.sharding import PartitionSpec as P

BLK = 128
BPD = 4
NZH, NX, NK = 4, 4, 2
NZL, NY = 4, 4
ROWS, COLS = NZH * NX * NK, NZL * NY
NA, NB = COLS * BPD, ROWS * BPD

time_step = 0.05
cell_side = 5.3
cutoff_sq = 6.25

MESH = pl.DeviceIdType.MESH
VMEM = pltpu.VMEM


class Place:
    def __init__(self):
        r, c = lax.axis_index("row"), lax.axis_index("col")
        self.r, self.c = r, c
        self.zh, self.x, self.k = r // (NX * NK), (r // NK) % NX, r % NK
        self.zl, self.y = c // NY, c % NY
        self.z_from = (self.zh + 3 - 2 * self.k) % NZH
        self.z_to = (self.zh + 1 + 2 * self.k) % NZH
        self.z_far = (self.zh + 2) % NZH
        self.x_mates = [(self.x + s) % NX for s in (2, 1, 3)]
        self.zl_mates = [(self.zl + s) % NZL for s in (2, 1, 3)]
        self.y_mates = [(self.y + s) % NY for s in (2, 1, 3)]

    def row_slot(self, zh, x, k):
        return (zh * NX + x) * NK + k

    def col_slot(self, zl, y):
        return zl * NY + y

    def at_z(self, zh):
        return (self.row_slot(zh, self.x, self.k), self.c)

    def at_x(self, x):
        return (self.row_slot(self.zh, x, self.k), self.c)

    def at_core(self):
        return (self.row_slot(self.zh, self.x, 1 - self.k), self.c)

    def at_zl(self, zl):
        return (self.r, self.col_slot(zl, self.y))

    def at_y(self, y):
        return (self.r, self.col_slot(self.zl, y))

    def partners(self):
        return (
            [self.at_z(self.z_from), self.at_z(self.z_to), self.at_core()]
            + [self.at_x(x) for x in self.x_mates]
            + [self.at_zl(z) for z in self.zl_mates]
            + [self.at_y(y) for y in self.y_mates]
        )


def greet(me):
    barrier = pltpu.get_barrier_semaphore()
    for device in me.partners():
        pl.semaphore_signal(barrier, inc=1, device_id=device, device_id_type=MESH)
    return barrier


def gather_kernel(pos, vel, old, kind, row_group, col_group, mine, send_sem, row_sem, col_sem):
    me = Place()
    barrier = greet(me)
    moved = pos[...] + time_step * vel[...] + 0.5 * time_step * time_step * old[...]
    kinds = kind[...]
    for e in range(BPD):
        mine[4 * e : 4 * e + 3, :] = moved[:, BLK * e : BLK * (e + 1)]
        mine[4 * e + 3 : 4 * e + 4, :] = kinds[e : e + 1, :]
    packet = mine[...]
    row_group[pl.ds(pl.multiple_of(me.c * 16, 16), 16), :] = packet
    col_group[pl.ds(pl.multiple_of(me.r * 16, 16), 16), :] = packet
    pl.semaphore_wait(barrier, len(me.partners()))

    started = []

    def ship(src, group, sems, slot, device):
        copy = pltpu.make_async_remote_copy(
            src_ref=src,
            dst_ref=group.at[pl.ds(pl.multiple_of(slot * 16, 16), 16), :],
            send_sem=send_sem.at[len(started)],
            recv_sem=sems.at[slot],
            device_id=device,
            device_id_type=MESH,
        )
        copy.start()
        started.append(copy)

    def arrived(group, sems, slot):
        view = group.at[pl.ds(pl.multiple_of(slot * 16, 16), 16), :]
        pltpu.make_async_remote_copy(
            src_ref=view,
            dst_ref=view,
            send_sem=send_sem.at[0],
            recv_sem=sems.at[slot],
            device_id=me.at_core(),
            device_id_type=MESH,
        ).wait_recv()
        return view

    own_row = me.row_slot(me.zh, me.x, me.k)
    for zh in (me.z_to, me.z_from):
        ship(mine, col_group, col_sem, own_row, me.at_z(zh))
    for zl in me.zl_mates:
        ship(mine, row_group, row_sem, me.c, me.at_zl(zl))
    for x in me.x_mates:
        ship(mine, col_group, col_sem, own_row, me.at_x(x))
    for y in me.y_mates:
        ship(mine, row_group, row_sem, me.c, me.at_y(y))
    ship(mine, col_group, col_sem, own_row, me.at_core())

    def spread(zh, relay):
        slot = me.row_slot(zh, me.x, me.k)
        view = arrived(col_group, col_sem, slot)
        if relay:
            ship(view, col_group, col_sem, slot, me.at_z(me.z_to))
        for x in me.x_mates:
            ship(view, col_group, col_sem, slot, me.at_x(x))
        ship(view, col_group, col_sem, slot, me.at_core())

    def share(zh, x):
        slot = me.row_slot(zh, x, me.k)
        view = arrived(col_group, col_sem, slot)
        ship(view, col_group, col_sem, slot, me.at_core())

    def fan_out(zl):
        slot = me.col_slot(zl, me.y)
        view = arrived(row_group, row_sem, slot)
        for y in me.y_mates:
            ship(view, row_group, row_sem, slot, me.at_y(y))

    for zl in me.zl_mates[1:]:
        fan_out(zl)
    for x in me.x_mates:
        share(me.zh, x)
    fan_out(me.zl_mates[0])
    spread(me.z_from, True)
    spread(me.z_to, False)
    for x in me.x_mates:
        share(me.z_from, x)
        share(me.z_to, x)
    spread(me.z_far, False)
    for x in me.x_mates:
        share(me.z_far, x)
    for y in me.y_mates:
        for zl in range(NZL):
            arrived(row_group, row_sem, me.col_slot(zl, y))
    for zh in range(NZH):
        for x in range(NX):
            arrived(col_group, col_sem, me.row_slot(zh, x, 1 - me.k))
    for copy in started:
        copy.wait_send()


def pair_kernel(
    box_y, box_z, pairs, live, sigma, epsilon, row_group, col_group, on_row, on_col, rows, cols, row_parts, col_parts
):
    sub = lax.broadcasted_iota(jnp.int32, (8, BLK), 0)
    lane = lax.broadcasted_iota(jnp.int32, (8, BLK), 1)
    sizes = jnp.zeros((8, BLK), jnp.float32)
    wells = jnp.zeros((8, BLK), jnp.float32)
    for n in range(sigma.shape[0]):
        sizes = jnp.where(lane == n, 0.5 * sigma[n], sizes)
        wells = jnp.where(lane == n, epsilon[n], wells)
    wells = math.sqrt(8.0) * jnp.sqrt(wells)
    kind_row = (sub == 3) | (sub == 7)

    def prepare(group, table, parts):
        def two_blocks(g, carry):
            both = group[pl.ds(pl.multiple_of(8 * g, 8), 8), :]
            low = jnp.min(both, axis=1, keepdims=True)
            high = jnp.max(both, axis=1, keepdims=True)
            center = jnp.broadcast_to(0.5 * (low + high), (8, BLK))
            near = both - center
            kinds = jnp.where(kind_row, both, 0.0).astype(jnp.int32)
            size = jnp.take_along_axis(sizes, kinds, axis=1, mode="promise_in_bounds")
            well = jnp.take_along_axis(wells, kinds, axis=1, mode="promise_in_bounds")
            for h in range(2):
                at = 4 * h
                tile = jnp.concatenate(
                    [near[at : at + 3], size[at + 3 : at + 4], well[at + 3 : at + 4], center[at : at + 3]], axis=0
                )
                table[2 * g + h] = tile
                coords = jnp.where(sub < 3, tile, jnp.where(sub == 3, 1.0, 0.0))
                head = coords.astype(jnp.bfloat16)
                tail = coords - head.astype(jnp.float32)
                parts[2 * g + h] = jnp.concatenate([head.astype(jnp.float32), tail], axis=0).astype(jnp.bfloat16)
            return carry

        lax.fori_loop(0, group.shape[0] // 8, two_blocks, 0, unroll=4)

    prepare(row_group, rows, row_parts)
    prepare(col_group, cols, col_parts)
    on_row[...] = jnp.zeros_like(on_row)
    on_col[...] = jnp.zeros_like(on_col)

    row_id, col_id = lax.axis_index("row"), lax.axis_index("col")
    box = jnp.where(sub == 5, BPD * cell_side, jnp.where(sub == 6, box_y, box_z))
    inverse_box = 1.0 / box

    def one_pair(p, carry):
        a, b = pairs[0, p], pairs[1, p]
        mine, theirs = rows[a], cols[b]
        apart = theirs - mine
        apart = apart - box * jnp.floor(apart * inverse_box + 0.5)
        shift = jnp.where(sub < 3, pltpu.roll(apart, 3, 0), 0.0)
        other = theirs + shift
        turned = mine.T
        heads, tails = [], []
        for n in range(0, BLK, 16):
            part = turned[n : n + 16]
            dx = other[0:1] - part[:, 0:1]
            dy = other[1:2] - part[:, 1:2]
            dz = other[2:3] - part[:, 2:3]
            sig = other[3:4] + part[:, 3:4]
            well = other[4:5] * part[:, 4:5]
            r2 = dx * dx + dy * dy + dz * dz
            sig2 = sig * sig
            soft = r2 + sig2
            guess = pl.reciprocal(soft, approx=True)
            inv = guess * (2.0 - soft * guess)
            ratio = sig2 * inv
            u3 = ratio * ratio * ratio
            w = jnp.maximum(1.0 - r2 * (1.0 / cutoff_sq), 0.0)
            lead = (3.0 - 6.0 * u3) * (inv * w)
            rest = (2.0 / cutoff_sq) - (2.0 / cutoff_sq) * u3
            k = (lead + rest) * (u3 * w * well)
            head = k.astype(jnp.bfloat16)
            heads.append(head)
            tails.append((k - head.astype(jnp.float32)).astype(jnp.bfloat16))
        head, tail = jnp.concatenate(heads, axis=0), jnp.concatenate(tails, axis=0)
        px, py = row_parts[a], col_parts[b]
        across = (((1,), (1,)), ((), ()))
        down = (((1,), (0,)), ((), ()))
        vr = lax.dot_general(py, head, across, preferred_element_type=jnp.float32) + lax.dot_general(
            py, tail, across, preferred_element_type=jnp.float32
        )
        vc = lax.dot_general(px, head, down, preferred_element_type=jnp.float32) + lax.dot_general(
            px, tail, down, preferred_element_type=jnp.float32
        )
        vr, vc = vr[0:8] + vr[8:16], vc[0:8] + vc[8:16]
        mine_r = px[0:8].astype(jnp.float32) + px[8:16].astype(jnp.float32)
        theirs_r = py[0:8].astype(jnp.float32) + py[8:16].astype(jnp.float32)
        fr = vr + (shift - mine_r) * vr[3:4]
        fc = vc - (shift + theirs_r) * vc[3:4]
        same = (b // BPD == row_id) & (a == col_id * BPD + b % BPD)
        fc = fc * jnp.where(same, 0.0, 1.0)
        on_row[a] = on_row[a] + fr[0:4]
        on_col[b] = on_col[b] + fc[0:4]
        return carry

    lax.fori_loop(0, live[0], one_pair, 0)


def scatter_kernel(
    on_row, on_col, old, vel, force, new_vel,
    core_in, x_out, x_in, z_out, z_relay, z_in, y_in, zl_out, zl_in,
    send_sem, core_sem, x_sem, z_sem, y_sem, zl_sem,
):
    me = Place()
    barrier = greet(me)
    pl.semaphore_wait(barrier, len(me.partners()))
    started = []

    def ship(src, dst, sem, device):
        copy = pltpu.make_async_remote_copy(
            src_ref=src, dst_ref=dst, send_sem=send_sem.at[len(started)], recv_sem=sem,
            device_id=device, device_id_type=MESH,
        )
        copy.start()
        started.append(copy)

    def arrived(dst, sem):
        pltpu.make_async_remote_copy(
            src_ref=dst, dst_ref=dst, send_sem=send_sem.at[0], recv_sem=sem,
            device_id=me.at_core(), device_id_type=MESH,
        ).wait_recv()

    xs = me.x_mates + [me.x]
    for x in xs:
        ship(on_col.at[:, x, 1 - me.k], core_in.at[x], core_sem.at[x], me.at_core())
    for y in me.y_mates:
        ship(on_row.at[:, y], y_in.at[me.y], y_sem.at[me.y], me.at_y(y))
    for x in me.x_mates:
        arrived(core_in.at[x], core_sem.at[x])
        x_out[x] = on_col[:, x, me.k] + core_in[x]
        ship(x_out.at[x], x_in.at[me.x], x_sem.at[me.x], me.at_x(x))
    arrived(core_in.at[me.x], core_sem.at[me.x])
    own = on_col[:, me.x, me.k] + core_in[me.x]

    total = on_row[:, me.y]
    for y in (me.y_mates[1], me.y_mates[2], me.y_mates[0]):
        arrived(y_in.at[y], y_sem.at[y])
        total = total + y_in[y]
    zl_out[...] = total
    for zl in me.zl_mates:
        ship(zl_out.at[zl], zl_in.at[me.zl], zl_sem.at[me.zl], me.at_zl(zl))

    for x in (me.x_mates[1], me.x_mates[2], me.x_mates[0]):
        arrived(x_in.at[x], x_sem.at[x])
        own = own + x_in[x]
    z_out[...] = own
    ship(z_out.at[me.z_far], z_in.at[0], z_sem.at[0], me.at_z(me.z_to))
    ship(z_out.at[me.z_from], z_in.at[1], z_sem.at[1], me.at_z(me.z_from))

    result = zl_out[me.zl] + z_out[me.zh]
    for zl in me.zl_mates:
        arrived(zl_in.at[zl], zl_sem.at[zl])
        result = result + zl_in[zl]
    arrived(z_in.at[0], z_sem.at[0])
    z_relay[...] = z_in[0] + z_out[me.z_to]
    ship(z_relay, z_in.at[2], z_sem.at[2], me.at_z(me.z_to))
    arrived(z_in.at[1], z_sem.at[1])
    result = result + z_in[1]
    arrived(z_in.at[2], z_sem.at[2])
    result = result + z_in[2]
    for e in range(BPD):
        force[:, BLK * e : BLK * (e + 1)] = result[e, 0:3]
    new_vel[...] = vel[...] + 0.5 * time_step * (old[...] + force[...])
    for copy in started:
        copy.wait_send()


def body(positions, velocities, old_forces, types, sigma_table, epsilon_table, pairs, live):
    f32 = jnp.float32
    dma = pltpu.SemaphoreType.DMA
    moved = positions + time_step * velocities + 0.5 * time_step * time_step * old_forces
    kinds = types.astype(f32).reshape(BPD, BLK)
    vmem = pl.BlockSpec(memory_space=VMEM)
    smem = pl.BlockSpec(memory_space=pltpu.SMEM)
    row_group, col_group = pl.pallas_call(
        gather_kernel,
        out_shape=(
            jax.ShapeDtypeStruct((NA * 4, BLK), f32),
            jax.ShapeDtypeStruct((NB * 4, BLK), f32),
        ),
        in_specs=[vmem] * 4,
        out_specs=(vmem, vmem),
        scratch_shapes=[VMEM((4 * BPD, BLK), f32), dma((48,)), dma((COLS,)), dma((ROWS,))],
        compiler_params=pltpu.CompilerParams(collective_id=0, has_side_effects=True),
        name="gather",
    )(positions, velocities, old_forces, kinds)

    def pair_call(*refs):
        return pair_kernel(ROWS * cell_side, COLS * cell_side, *refs)

    on_row, on_col = pl.pallas_call(
        pair_call,
        out_shape=(
            jax.ShapeDtypeStruct((NA, 4, BLK), f32),
            jax.ShapeDtypeStruct((NB, 4, BLK), f32),
        ),
        in_specs=[smem] * 4 + [vmem] * 2,
        out_specs=(vmem, vmem),
        scratch_shapes=[
            VMEM((NA, 8, BLK), f32),
            VMEM((NB, 8, BLK), f32),
            VMEM((NA, 16, BLK), jnp.bfloat16),
            VMEM((NB, 16, BLK), jnp.bfloat16),
        ],
        name="pairs",
    )(pairs.reshape(2, -1), live.reshape(1), sigma_table, epsilon_table, row_group, col_group)

    tile = (BPD, 4, BLK)
    new_forces, new_velocities = pl.pallas_call(
        scatter_kernel,
        out_shape=(jax.ShapeDtypeStruct(positions.shape, f32), jax.ShapeDtypeStruct(positions.shape, f32)),
        in_specs=[vmem] * 4,
        out_specs=(vmem, vmem),
        scratch_shapes=[
            VMEM((NX, NZH) + tile, f32),
            VMEM((NX, NZH) + tile, f32),
            VMEM((NX, NZH) + tile, f32),
            VMEM((NZH,) + tile, f32),
            VMEM(tile, f32),
            VMEM((3,) + tile, f32),
            VMEM((NY, NZL) + tile, f32),
            VMEM((NZL,) + tile, f32),
            VMEM((NZL,) + tile, f32),
            dma((16,)),
            dma((NX,)),
            dma((NX,)),
            dma((3,)),
            dma((NY,)),
            dma((NZL,)),
        ],
        compiler_params=pltpu.CompilerParams(collective_id=1, has_side_effects=True),
        name="scatter",
    )(
        on_row.reshape((NZL, NY) + tile),
        on_col.reshape((NZH, NX, NK) + tile),
        old_forces,
        velocities,
    )
    return moved, new_velocities, new_forces


def solution(mesh):
    in_specs = (
        P(None, ("row", "col")),
        P(None, ("row", "col")),
        P(None, ("row", "col")),
        P(("row", "col")),
        P(),
        P(),
        P("row", "col", None, None),
        P("row", "col"),
    )
    out_specs = (P(None, ("row", "col")), P(None, ("row", "col")), P(None, ("row", "col")))
    return jax.shard_map(body, mesh=mesh, in_specs=in_specs, out_specs=out_specs, check_vma=False)
```

```python
import math

import jax
import jax.numpy as jnp
from jax import lax
from jax.experimental import pallas as pl
from jax.experimental.pallas import tpu as pltpu
from jax.sharding import PartitionSpec as P

BLK = 128
BPD = 4
NZH, NX, NK = 4, 4, 2
NZL, NY = 4, 4
ROWS, COLS = NZH * NX * NK, NZL * NY
NA, NB = COLS * BPD, ROWS * BPD

time_step = 0.05
cell_side = 5.3
cutoff_sq = 6.25

MESH = pl.DeviceIdType.MESH
VMEM = pltpu.VMEM


class Place:
    def __init__(self):
        r, c = lax.axis_index("row"), lax.axis_index("col")
        self.r, self.c = r, c
        self.zh, self.x, self.k = r // (NX * NK), (r // NK) % NX, r % NK
        self.zl, self.y = c // NY, c % NY
        self.z_from = (self.zh + 3 - 2 * self.k) % NZH
        self.z_to = (self.zh + 1 + 2 * self.k) % NZH
        self.z_far = (self.zh + 2) % NZH
        self.x_mates = [(self.x + s) % NX for s in (2, 1, 3)]
        self.zl_mates = [(self.zl + s) % NZL for s in (2, 1, 3)]
        self.y_mates = [(self.y + s) % NY for s in (2, 1, 3)]

    def row_slot(self, zh, x, k):
        return (zh * NX + x) * NK + k

    def col_slot(self, zl, y):
        return zl * NY + y

    def at_z(self, zh):
        return (self.row_slot(zh, self.x, self.k), self.c)

    def at_x(self, x):
        return (self.row_slot(self.zh, x, self.k), self.c)

    def at_core(self):
        return (self.row_slot(self.zh, self.x, 1 - self.k), self.c)

    def at_zl(self, zl):
        return (self.r, self.col_slot(zl, self.y))

    def at_y(self, y):
        return (self.r, self.col_slot(self.zl, y))

    def partners(self):
        return (
            [self.at_z(self.z_from), self.at_z(self.z_to), self.at_core()]
            + [self.at_x(x) for x in self.x_mates]
            + [self.at_zl(z) for z in self.zl_mates]
            + [self.at_y(y) for y in self.y_mates]
        )


def greet(me):
    barrier = pltpu.get_barrier_semaphore()
    for device in me.partners():
        pl.semaphore_signal(barrier, inc=1, device_id=device, device_id_type=MESH)
    return barrier


def gather_kernel(pos, vel, old, kind, row_group, col_group, mine, send_sem, row_sem, col_sem):
    me = Place()
    barrier = greet(me)
    moved = pos[...] + time_step * vel[...] + 0.5 * time_step * time_step * old[...]
    kinds = kind[...].astype(jnp.float32)
    for e in range(BPD):
        mine[4 * e : 4 * e + 3, :] = moved[:, BLK * e : BLK * (e + 1)]
        mine[4 * e + 3 : 4 * e + 4, :] = kinds[e : e + 1, :]
    packet = mine[...]
    row_group[pl.ds(pl.multiple_of(me.c * 16, 16), 16), :] = packet
    col_group[pl.ds(pl.multiple_of(me.r * 16, 16), 16), :] = packet
    pl.semaphore_wait(barrier, len(me.partners()))

    started = []

    def ship(src, group, sems, slot, device):
        copy = pltpu.make_async_remote_copy(
            src_ref=src,
            dst_ref=group.at[pl.ds(pl.multiple_of(slot * 16, 16), 16), :],
            send_sem=send_sem.at[len(started)],
            recv_sem=sems.at[slot],
            device_id=device,
            device_id_type=MESH,
        )
        copy.start()
        started.append(copy)

    def arrived(group, sems, slot):
        view = group.at[pl.ds(pl.multiple_of(slot * 16, 16), 16), :]
        pltpu.make_async_remote_copy(
            src_ref=view,
            dst_ref=view,
            send_sem=send_sem.at[0],
            recv_sem=sems.at[slot],
            device_id=me.at_core(),
            device_id_type=MESH,
        ).wait_recv()
        return view

    own_row = me.row_slot(me.zh, me.x, me.k)
    for zh in (me.z_to, me.z_from):
        ship(mine, col_group, col_sem, own_row, me.at_z(zh))
    for zl in me.zl_mates:
        ship(mine, row_group, row_sem, me.c, me.at_zl(zl))
    for x in me.x_mates:
        ship(mine, col_group, col_sem, own_row, me.at_x(x))
    for y in me.y_mates:
        ship(mine, row_group, row_sem, me.c, me.at_y(y))
    ship(mine, col_group, col_sem, own_row, me.at_core())

    def spread(zh, relay):
        slot = me.row_slot(zh, me.x, me.k)
        view = arrived(col_group, col_sem, slot)
        if relay:
            ship(view, col_group, col_sem, slot, me.at_z(me.z_to))
        for x in me.x_mates:
            ship(view, col_group, col_sem, slot, me.at_x(x))
        ship(view, col_group, col_sem, slot, me.at_core())

    def share(zh, x):
        slot = me.row_slot(zh, x, me.k)
        view = arrived(col_group, col_sem, slot)
        ship(view, col_group, col_sem, slot, me.at_core())

    def fan_out(zl):
        slot = me.col_slot(zl, me.y)
        view = arrived(row_group, row_sem, slot)
        for y in me.y_mates:
            ship(view, row_group, row_sem, slot, me.at_y(y))

    for zl in me.zl_mates[1:]:
        fan_out(zl)
    for x in me.x_mates:
        share(me.zh, x)
    fan_out(me.zl_mates[0])
    spread(me.z_from, True)
    spread(me.z_to, False)
    for x in me.x_mates:
        share(me.z_from, x)
        share(me.z_to, x)
    spread(me.z_far, False)
    for x in me.x_mates:
        share(me.z_far, x)
    for y in me.y_mates:
        for zl in range(NZL):
            arrived(row_group, row_sem, me.col_slot(zl, y))
    for zh in range(NZH):
        for x in range(NX):
            arrived(col_group, col_sem, me.row_slot(zh, x, 1 - me.k))
    for copy in started:
        copy.wait_send()


def split3(v):
    head = v.astype(jnp.bfloat16).astype(jnp.float32)
    rest = v - head
    mid = rest.astype(jnp.bfloat16).astype(jnp.float32)
    return head, mid, rest - mid


def pair_kernel(
    box_y, box_z, pairs, live, sigma, epsilon, row_group, col_group, pos, vel, old, on_row, on_col, moved,
    rows, cols, row_mid, col_mid, row_acc, col_acc, listed, todo, terms, k_head, k_tail, sem,
):
    f32, bf16 = jnp.float32, jnp.bfloat16
    moved[...] = pos[...] + time_step * vel[...] + 0.5 * time_step * time_step * old[...]
    sub = lax.broadcasted_iota(jnp.int32, (8, BLK), 0)
    lane = lax.broadcasted_iota(jnp.int32, (8, BLK), 1)
    sizes = jnp.zeros((8, BLK), f32)
    wells = jnp.zeros((8, BLK), f32)
    for n in range(sigma.shape[0]):
        sizes = jnp.where(lane == n, 0.5 * sigma[n], sizes)
        wells = jnp.where(lane == n, epsilon[n], wells)
    wells = math.sqrt(16.0 / cutoff_sq) * jnp.sqrt(wells)
    kind_row = (sub == 3) | (sub == 7)
    box = jnp.where(sub == 0, BPD * cell_side, jnp.where(sub == 1, box_y, jnp.where(sub == 2, box_z, 1.0)))
    inverse_box = 1.0 / box

    def wrap(v):
        return v - box * jnp.floor(v * inverse_box + 0.5)

    def prepare(group, table, middle):
        def two_blocks(g, bounds):
            both = group[pl.ds(pl.multiple_of(8 * g, 8), 8), :]
            low = jnp.broadcast_to(jnp.min(both, axis=1, keepdims=True), (8, BLK))
            high = jnp.broadcast_to(jnp.max(both, axis=1, keepdims=True), (8, BLK))
            center = 0.5 * (low + high)
            near = both - center
            kinds = jnp.where(kind_row, both, 0.0).astype(jnp.int32)
            size = jnp.take_along_axis(sizes, kinds, axis=1, mode="promise_in_bounds")
            well = pltpu.roll(jnp.take_along_axis(wells, kinds, axis=1, mode="promise_in_bounds"), 1, 0)
            mixed = jnp.where(kind_row, size, near)
            for h in range(2):
                part = mixed if h == 0 else pltpu.roll(mixed, 4, 0)
                deep = well if h == 0 else pltpu.roll(well, 4, 0)
                mid = center if h == 0 else pltpu.roll(center, 4, 0)
                table[2 * g + h] = jnp.where(sub < 4, part, jnp.where(sub == 4, deep, 0.0))
                middle[2 * g + h] = jnp.where(sub < 3, mid, 0.0)
            here = lane == g
            return jnp.where(here, low, bounds[0]), jnp.where(here, high, bounds[1])

        start = group[0:8, :]
        return lax.fori_loop(0, group.shape[0] // 8, two_blocks, (start, start), unroll=4)

    row_low, row_high = prepare(row_group, rows, row_mid)
    col_low, col_high = prepare(col_group, cols, col_mid)

    firsts = jnp.broadcast_to(pairs[0:1, :], (8, BLK))
    seconds = jnp.broadcast_to(pairs[1:2, :], (8, BLK))

    def pick(bound, index):
        got = jnp.take_along_axis(bound, index >> 1, axis=1, mode="promise_in_bounds")
        return jnp.where((index & 1) == 1, pltpu.roll(got, 4, 0), got)

    xl, xh = pick(row_low, firsts), pick(row_high, firsts)
    yl, yh = pick(col_low, seconds), pick(col_high, seconds)
    apart = wrap(jnp.where(sub < 3, 0.5 * ((yl + yh) - (xl + xh)), 0.0))
    gap = jnp.abs(apart) - 0.5 * ((yh - yl) + (xh - xl))
    gap = jnp.where(sub < 3, jnp.maximum(gap, 0.0), 0.0)
    gap2 = jnp.sum(gap * gap, axis=0, keepdims=True)
    near_by = jnp.broadcast_to(gap2, (8, BLK)) < cutoff_sq + 0.01
    active = jnp.where(near_by & (lane < live[0, 0]), 1.0, 0.0)
    big_sub = lax.broadcasted_iota(jnp.int32, (BLK, BLK), 0)
    big_lane = lax.broadcasted_iota(jnp.int32, (BLK, BLK), 1)
    across = (((1,), (1,)), ((), ()))
    down = (((1,), (0,)), ((), ()))

    def dot(u, v, dims):
        return lax.dot_general(u, v, dims, preferred_element_type=f32)

    upto = dot(jnp.where(big_lane <= big_sub, 1.0, 0.0).astype(bf16), active.astype(bf16), across)[:, 0:1]
    before = dot(jnp.where(big_lane < big_sub, 1.0, 0.0).astype(bf16), active.astype(bf16), across)[:, 0:1]
    place = big_lane.astype(f32)
    move = jnp.where((place >= before) & (place < upto), 1.0, 0.0).astype(bf16)
    both = jnp.where(sub == 0, firsts, seconds).astype(f32).astype(bf16)
    packed = dot(both, move, down)
    count = jnp.broadcast_to(jnp.sum(active, axis=1, keepdims=True), (8, BLK))
    spare = jnp.where(sub == 0, float(NA), float(NB))
    packed = jnp.where(lane.astype(f32) < count, packed, spare)
    listed[...] = jnp.where(sub == 2, count, packed).astype(jnp.int32)
    copy = pltpu.make_async_copy(listed, todo, sem)
    copy.start()
    row_acc[...] = jnp.zeros_like(row_acc)
    col_acc[...] = jnp.zeros_like(col_acc)
    copy.wait()
    total = todo[2, 0]
    row_id, col_id = lax.axis_index("row"), lax.axis_index("col")
    scale = 1.5 * cutoff_sq

    def force_sources(tile):
        well = tile[4:5]
        v = jnp.where(sub < 3, tile * well, jnp.where(sub == 3, well, 0.0))
        head, mid, low = split3(v)
        first = jnp.where(sub < 4, head, pltpu.roll(low, 4, 0))
        return jnp.concatenate([first, mid], axis=0).astype(bf16)

    def fold(v):
        v = v[0:8] + v[8:16]
        return v + pltpu.roll(v, 4, 0)

    def turn(p, carry):
        a1, b1, a2, b2, shift1, shift2 = carry
        mine, theirs = rows[a2], cols[b2]
        px, py = force_sources(mine), force_sources(theirs)
        head, tail = k_head[...], k_tail[...]
        vr = fold(dot(py, head, across) + dot(py, tail, across))
        vc = fold(dot(px, head, down) + dot(px, tail, down))
        fr = (vr + (shift2 - mine) * vr[3:4]) * mine[4:5]
        fc = (vc - (shift2 + theirs) * vc[3:4]) * theirs[4:5]
        same = (b2 // BPD == row_id) & (a2 == col_id * BPD + b2 % BPD)
        fc = fc * jnp.where(same, 0.0, 1.0)
        row_acc[a2] = row_acc[a2] + fr
        col_acc[b2] = col_acc[b2] + fc
        for n in range(0, BLK, 16):
            w = jnp.maximum(terms[n : n + 16, 0:BLK], 0.0)
            soft = terms[n : n + 16, BLK : 2 * BLK]
            sig2 = terms[n : n + 16, 2 * BLK : 3 * BLK]
            guess = pl.reciprocal(soft, approx=True)
            inv = guess * (2.0 - soft * guess)
            ratio = sig2 * inv
            u3 = ratio * ratio * ratio
            t = inv * w
            t1 = t + 1.0
            k = (t1 - u3 * (t1 + t)) * (u3 * w)
            high = k.astype(bf16)
            k_head[n : n + 16, :] = high
            k_tail[n : n + 16, :] = (k - high.astype(f32)).astype(bf16)
        valid = p < total
        q = jnp.minimum(p, BLK - 1)
        a, b = jnp.where(valid, todo[0, q], NA), jnp.where(valid, todo[1, q], NB)
        mine, theirs = rows[a], cols[b]
        shift = wrap(col_mid[b] - row_mid[a])
        other = theirs + shift
        sq = mine * mine
        norm = (sq[0:1] + sq[1:2] + sq[2:3]) * (1.0 / cutoff_sq)
        left = jnp.where(
            sub < 5, mine, jnp.where(sub == 5, norm, jnp.where(sub == 6, sq[3:4], 1.0))
        )
        head, mid, low = split3(left)
        left = jnp.concatenate([head, head, head, mid, mid, low], axis=0).T.astype(bf16)
        sq = other * other
        norm = sq[0:1] + sq[1:2] + sq[2:3]
        size2 = sq[3:4]
        inv_c = 1.0 / scale
        for_w = jnp.where(
            sub < 3, other * (2.0 / cutoff_sq),
            jnp.where(sub == 5, -1.0, jnp.where(sub == 7, 1.0 - norm * (1.0 / cutoff_sq), 0.0)),
        )
        for_sig = jnp.where(
            sub == 3, other * (2.0 * inv_c), jnp.where(sub == 6, inv_c, jnp.where(sub == 7, size2 * inv_c, 0.0))
        )
        for_soft = jnp.where(
            sub < 3, other * (-2.0 * inv_c),
            jnp.where(sub == 5, cutoff_sq * inv_c, jnp.where(sub == 7, (norm + size2) * inv_c, for_sig)),
        )
        for n, right in enumerate((for_w, for_soft, for_sig)):
            head, mid, low = split3(right)
            right = jnp.concatenate([head, mid, low, head, mid, head], axis=0).astype(bf16)
            terms[:, n * BLK : (n + 1) * BLK] = dot(left, right, down)
        return a, b, a1, b1, shift, shift1

    none = row_acc[0]
    spare_a, spare_b = jnp.int32(NA), jnp.int32(NB)
    lax.fori_loop(0, total + 2, turn, (spare_a, spare_b, spare_a, spare_b, none, none))
    on_row[...] = row_acc[0:NA, 0:4, :]
    on_col[...] = col_acc[0:NB, 0:4, :]


def scatter_kernel(
    on_row, on_col, row_share, col_share,
    core_in, x_out, x_in, z_out, z_relay, z_in, y_in, zl_out, zl_in,
    send_sem, core_sem, x_sem, z_sem, y_sem, zl_sem,
):
    me = Place()
    barrier = greet(me)
    pl.semaphore_wait(barrier, len(me.partners()))
    started = []

    def ship(src, dst, sem, device):
        copy = pltpu.make_async_remote_copy(
            src_ref=src, dst_ref=dst, send_sem=send_sem.at[len(started)], recv_sem=sem,
            device_id=device, device_id_type=MESH,
        )
        copy.start()
        started.append(copy)

    def arrived(dst, sem):
        pltpu.make_async_remote_copy(
            src_ref=dst, dst_ref=dst, send_sem=send_sem.at[0], recv_sem=sem,
            device_id=me.at_core(), device_id_type=MESH,
        ).wait_recv()

    xs = me.x_mates + [me.x]
    for x in xs:
        ship(on_col.at[:, x, 1 - me.k], core_in.at[x], core_sem.at[x], me.at_core())
    for y in me.y_mates:
        ship(on_row.at[:, y], y_in.at[me.y], y_sem.at[me.y], me.at_y(y))
    for x in me.x_mates:
        arrived(core_in.at[x], core_sem.at[x])
        x_out[x] = on_col[:, x, me.k] + core_in[x]
        ship(x_out.at[x], x_in.at[me.x], x_sem.at[me.x], me.at_x(x))
    arrived(core_in.at[me.x], core_sem.at[me.x])
    own = on_col[:, me.x, me.k] + core_in[me.x]

    total = on_row[:, me.y]
    for y in (me.y_mates[1], me.y_mates[2], me.y_mates[0]):
        arrived(y_in.at[y], y_sem.at[y])
        total = total + y_in[y]
    zl_out[...] = total
    for zl in me.zl_mates:
        ship(zl_out.at[zl], zl_in.at[me.zl], zl_sem.at[me.zl], me.at_zl(zl))

    for x in (me.x_mates[1], me.x_mates[2], me.x_mates[0]):
        arrived(x_in.at[x], x_sem.at[x])
        own = own + x_in[x]
    z_out[...] = own
    ship(z_out.at[me.z_far], z_in.at[0], z_sem.at[0], me.at_z(me.z_to))
    ship(z_out.at[me.z_from], z_in.at[1], z_sem.at[1], me.at_z(me.z_from))

    row_total, col_total = zl_out[me.zl], z_out[me.zh]
    for zl in me.zl_mates:
        arrived(zl_in.at[zl], zl_sem.at[zl])
        row_total = row_total + zl_in[zl]
    for e in range(BPD):
        row_share[:, BLK * e : BLK * (e + 1)] = row_total[e, 0:3]
    arrived(z_in.at[0], z_sem.at[0])
    z_relay[...] = z_in[0] + z_out[me.z_to]
    ship(z_relay, z_in.at[2], z_sem.at[2], me.at_z(me.z_to))
    arrived(z_in.at[1], z_sem.at[1])
    col_total = col_total + z_in[1]
    arrived(z_in.at[2], z_sem.at[2])
    col_total = col_total + z_in[2]
    for e in range(BPD):
        col_share[:, BLK * e : BLK * (e + 1)] = col_total[e, 0:3]
    for copy in started:
        copy.wait_send()


def body(positions, velocities, old_forces, types, sigma_table, epsilon_table, pairs, live):
    f32 = jnp.float32
    dma = pltpu.SemaphoreType.DMA
    kinds = types.reshape(BPD, BLK)
    vmem = pl.BlockSpec(memory_space=VMEM)
    smem = pl.BlockSpec(memory_space=pltpu.SMEM)
    row_group, col_group = pl.pallas_call(
        gather_kernel,
        out_shape=(
            jax.ShapeDtypeStruct((NA * 4, BLK), f32),
            jax.ShapeDtypeStruct((NB * 4, BLK), f32),
        ),
        in_specs=[vmem] * 4,
        out_specs=(vmem, vmem),
        scratch_shapes=[VMEM((4 * BPD, BLK), f32), dma((48,)), dma((COLS,)), dma((ROWS,))],
        compiler_params=pltpu.CompilerParams(collective_id=0, has_side_effects=True),
        name="gather",
    )(positions, velocities, old_forces, kinds)

    def pair_call(*refs):
        return pair_kernel(ROWS * cell_side, COLS * cell_side, *refs)

    on_row, on_col, moved = pl.pallas_call(
        pair_call,
        out_shape=(
            jax.ShapeDtypeStruct((NA, 4, BLK), f32),
            jax.ShapeDtypeStruct((NB, 4, BLK), f32),
            jax.ShapeDtypeStruct(positions.shape, f32),
        ),
        in_specs=[vmem] + [smem] * 3 + [vmem] * 5,
        out_specs=(vmem, vmem, vmem),
        scratch_shapes=[
            VMEM((NA + 1, 8, BLK), f32),
            VMEM((NB + 1, 8, BLK), f32),
            VMEM((NA + 1, 8, BLK), f32),
            VMEM((NB + 1, 8, BLK), f32),
            VMEM((NA + 1, 8, BLK), f32),
            VMEM((NB + 1, 8, BLK), f32),
            VMEM((8, BLK), jnp.int32),
            pltpu.SMEM((8, BLK), jnp.int32),
            VMEM((BLK, 3 * BLK), f32),
            VMEM((BLK, BLK), jnp.bfloat16),
            VMEM((BLK, BLK), jnp.bfloat16),
            dma,
        ],
        name="pairs",
    )(
        pairs.reshape(2, -1), live, sigma_table, epsilon_table, row_group, col_group,
        positions, velocities, old_forces,
    )

    tile = (BPD, 4, BLK)
    row_share, col_share = pl.pallas_call(
        scatter_kernel,
        out_shape=(jax.ShapeDtypeStruct(positions.shape, f32), jax.ShapeDtypeStruct(positions.shape, f32)),
        in_specs=[vmem] * 2,
        out_specs=(vmem, vmem),
        scratch_shapes=[
            VMEM((NX, NZH) + tile, f32),
            VMEM((NX, NZH) + tile, f32),
            VMEM((NX, NZH) + tile, f32),
            VMEM((NZH,) + tile, f32),
            VMEM(tile, f32),
            VMEM((3,) + tile, f32),
            VMEM((NY, NZL) + tile, f32),
            VMEM((NZL,) + tile, f32),
            VMEM((NZL,) + tile, f32),
            dma((16,)),
            dma((NX,)),
            dma((NX,)),
            dma((3,)),
            dma((NY,)),
            dma((NZL,)),
        ],
        compiler_params=pltpu.CompilerParams(collective_id=1, has_side_effects=True),
        name="scatter",
    )(
        on_row.reshape((NZL, NY) + tile),
        on_col.reshape((NZH, NX, NK) + tile),
    )
    new_forces = row_share + col_share
    new_velocities = velocities + 0.5 * time_step * (old_forces + new_forces)
    return moved, new_velocities, new_forces


def solution(mesh):
    in_specs = (
        P(None, ("row", "col")),
        P(None, ("row", "col")),
        P(None, ("row", "col")),
        P(("row", "col")),
        P(),
        P(),
        P("row", "col", None, None),
        P("row", "col"),
    )
    out_specs = (P(None, ("row", "col")), P(None, ("row", "col")), P(None, ("row", "col")))
    return jax.shard_map(body, mesh=mesh, in_specs=in_specs, out_specs=out_specs, check_vma=False)
```

```python
import math

import jax
import jax.numpy as jnp
from jax import lax
from jax.experimental import pallas as pl
from jax.experimental.pallas import tpu as pltpu
from jax.sharding import PartitionSpec as P

BLK = 128
BPD = 4
NZH, NX, NK = 4, 4, 2
NZL, NY = 4, 4
ROWS, COLS = NZH * NX * NK, NZL * NY
NA, NB = COLS * BPD, ROWS * BPD

time_step = 0.05
cell_side = 5.3
cutoff_sq = 6.25

MESH = pl.DeviceIdType.MESH
VMEM = pltpu.VMEM


class Place:
    def __init__(self):
        r, c = lax.axis_index("row"), lax.axis_index("col")
        self.r, self.c = r, c
        self.zh, self.x, self.k = r // (NX * NK), (r // NK) % NX, r % NK
        self.zl, self.y = c // NY, c % NY
        self.z_from = (self.zh + 3 - 2 * self.k) % NZH
        self.z_to = (self.zh + 1 + 2 * self.k) % NZH
        self.z_far = (self.zh + 2) % NZH
        self.x_mates = [(self.x + s) % NX for s in (2, 1, 3)]
        self.zl_mates = [(self.zl + s) % NZL for s in (2, 1, 3)]
        self.y_mates = [(self.y + s) % NY for s in (2, 1, 3)]

    def row_slot(self, zh, x, k):
        return (zh * NX + x) * NK + k

    def col_slot(self, zl, y):
        return zl * NY + y

    def at_z(self, zh):
        return (self.row_slot(zh, self.x, self.k), self.c)

    def at_x(self, x):
        return (self.row_slot(self.zh, x, self.k), self.c)

    def at_x_other(self, x):
        return (self.row_slot(self.zh, x, 1 - self.k), self.c)

    def at_core(self):
        return (self.row_slot(self.zh, self.x, 1 - self.k), self.c)

    def at_zl(self, zl):
        return (self.r, self.col_slot(zl, self.y))

    def at_y(self, y):
        return (self.r, self.col_slot(self.zl, y))

    def partners(self):
        return (
            [self.at_z(self.z_from), self.at_z(self.z_to), self.at_core()]
            + [self.at_x(x) for x in self.x_mates]
            + [self.at_x_other(x) for x in self.x_mates]
            + [self.at_zl(z) for z in self.zl_mates]
            + [self.at_y(y) for y in self.y_mates]
        )


def greet(me):
    barrier = pltpu.get_barrier_semaphore()
    for device in me.partners():
        pl.semaphore_signal(barrier, inc=1, device_id=device, device_id_type=MESH)
    return barrier


def gather_kernel(
    pos_hbm, vel_hbm, old_hbm, kind_hbm, sigma_hbm, epsilon_hbm, pairs_hbm, live_hbm,
    row_group, col_group, moved, pairs, tables,
    pos, vel, old, kind, sigma, epsilon, live, mine, local_sem, send_sem, row_sem, col_sem,
):
    me = Place()
    barrier = greet(me)
    local = [
        pltpu.make_async_copy(src, dst, local_sem.at[n])
        for n, (src, dst) in enumerate(
            (
                (pos_hbm, pos), (vel_hbm, vel), (old_hbm, old), (kind_hbm, kind),
                (sigma_hbm, sigma), (epsilon_hbm, epsilon), (live_hbm, live), (pairs_hbm, pairs),
            )
        )
    ]
    for copy in local:
        copy.start()
    for copy in local[:4]:
        copy.wait()
    moved[...] = pos[...] + time_step * vel[...] + 0.5 * time_step * time_step * old[...]
    kinds = kind[...].astype(jnp.float32)
    for e in range(BPD):
        mine[4 * e : 4 * e + 3, :] = moved[:, BLK * e : BLK * (e + 1)]
        mine[4 * e + 3 : 4 * e + 4, :] = kinds[e : e + 1, :]
    packet = mine[...]
    row_group[pl.ds(pl.multiple_of(me.c * 16, 16), 16), :] = packet
    col_group[pl.ds(pl.multiple_of(me.r * 16, 16), 16), :] = packet
    pl.semaphore_wait(barrier, len(me.partners()))

    started = []

    def ship(src, group, sems, slot, device):
        copy = pltpu.make_async_remote_copy(
            src_ref=src,
            dst_ref=group.at[pl.ds(pl.multiple_of(slot * 16, 16), 16), :],
            send_sem=send_sem.at[len(started)],
            recv_sem=sems.at[slot],
            device_id=device,
            device_id_type=MESH,
        )
        copy.start()
        started.append(copy)

    def arrived(group, sems, slot):
        view = group.at[pl.ds(pl.multiple_of(slot * 16, 16), 16), :]
        pltpu.make_async_remote_copy(
            src_ref=view,
            dst_ref=view,
            send_sem=send_sem.at[0],
            recv_sem=sems.at[slot],
            device_id=me.at_core(),
            device_id_type=MESH,
        ).wait_recv()
        return view

    own_row = me.row_slot(me.zh, me.x, me.k)
    for zh in (me.z_to, me.z_from):
        ship(mine, col_group, col_sem, own_row, me.at_z(zh))
    for zl in me.zl_mates:
        ship(mine, row_group, row_sem, me.c, me.at_zl(zl))
    for x in me.x_mates:
        ship(mine, col_group, col_sem, own_row, me.at_x(x))
    for y in me.y_mates:
        ship(mine, row_group, row_sem, me.c, me.at_y(y))
    ship(mine, col_group, col_sem, own_row, me.at_core())

    for copy in local[4:]:
        copy.wait()
    lane = lax.broadcasted_iota(jnp.int32, (8, BLK), 1)
    sizes = jnp.zeros((8, BLK), jnp.float32)
    wells = jnp.zeros((8, BLK), jnp.float32)
    for n in range(sigma.shape[0]):
        sizes = jnp.where(lane == n, 0.5 * sigma[n], sizes)
        wells = jnp.where(lane == n, epsilon[n], wells)
    tables[0] = sizes
    tables[1] = math.sqrt(16.0 / cutoff_sq) * jnp.sqrt(wells)
    tables[2] = jnp.full((8, BLK), live[0, 0].astype(jnp.float32))

    def spread(zh, relay=False, last=False):
        slot = me.row_slot(zh, me.x, me.k)
        view = arrived(col_group, col_sem, slot)
        if relay:
            ship(view, col_group, col_sem, slot, me.at_z(me.z_to))
        for x in me.x_mates:
            ship(view, col_group, col_sem, slot, me.at_x(x))
            if last:
                ship(view, col_group, col_sem, slot, me.at_x_other(x))
        ship(view, col_group, col_sem, slot, me.at_core())

    def share(zh, x):
        slot = me.row_slot(zh, x, me.k)
        view = arrived(col_group, col_sem, slot)
        ship(view, col_group, col_sem, slot, me.at_core())

    def fan_out(zl):
        slot = me.col_slot(zl, me.y)
        view = arrived(row_group, row_sem, slot)
        for y in me.y_mates:
            ship(view, row_group, row_sem, slot, me.at_y(y))

    for zl in me.zl_mates[1:]:
        fan_out(zl)
    for x in me.x_mates:
        share(me.zh, x)
    fan_out(me.zl_mates[0])
    spread(me.z_from, relay=True)
    spread(me.z_to)
    for x in me.x_mates:
        share(me.z_from, x)
        share(me.z_to, x)
    spread(me.z_far, last=True)
    for x in me.x_mates:
        arrived(col_group, col_sem, me.row_slot(me.z_far, x, me.k))
    for y in me.y_mates:
        for zl in range(NZL):
            arrived(row_group, row_sem, me.col_slot(zl, y))
    for zh in range(NZH):
        for x in range(NX):
            arrived(col_group, col_sem, me.row_slot(zh, x, 1 - me.k))
    for copy in started:
        copy.wait_send()


def split3(v):
    head = v.astype(jnp.bfloat16).astype(jnp.float32)
    rest = v - head
    mid = rest.astype(jnp.bfloat16).astype(jnp.float32)
    return head, mid, rest - mid


def pair_kernel(
    box_y, box_z, pairs, tables, row_group, col_group, moved_in, on_row, on_col, moved,
    rows, cols, row_mid, col_mid, row_acc, col_acc, listed, todo, k_parts, lefts, rights, sources, sem,
):
    f32, bf16 = jnp.float32, jnp.bfloat16
    moved[...] = moved_in[...]
    row_acc[...] = jnp.zeros_like(row_acc)
    col_acc[...] = jnp.zeros_like(col_acc)
    sub = lax.broadcasted_iota(jnp.int32, (8, BLK), 0)
    lane = lax.broadcasted_iota(jnp.int32, (8, BLK), 1)
    sizes, wells = tables[0], tables[1]
    kind_row = (sub == 3) | (sub == 7)
    box = jnp.where(sub == 0, BPD * cell_side, jnp.where(sub == 1, box_y, jnp.where(sub == 2, box_z, 1.0)))
    inverse_box = 1.0 / box

    def wrap(v):
        return v - box * jnp.floor(v * inverse_box + 0.5)

    def prepare(group, table, middle):
        def two_blocks(g, bounds):
            both = group[pl.ds(pl.multiple_of(8 * g, 8), 8), :]
            low = jnp.broadcast_to(jnp.min(both, axis=1, keepdims=True), (8, BLK))
            high = jnp.broadcast_to(jnp.max(both, axis=1, keepdims=True), (8, BLK))
            center = 0.5 * (low + high)
            near = both - center
            kinds = jnp.where(kind_row, both, 0.0).astype(jnp.int32)
            size = jnp.take_along_axis(sizes, kinds, axis=1, mode="promise_in_bounds")
            well = pltpu.roll(jnp.take_along_axis(wells, kinds, axis=1, mode="promise_in_bounds"), 1, 0)
            mixed = jnp.where(kind_row, size, near)
            for h in range(2):
                part = mixed if h == 0 else pltpu.roll(mixed, 4, 0)
                deep = well if h == 0 else pltpu.roll(well, 4, 0)
                mid = center if h == 0 else pltpu.roll(center, 4, 0)
                table[2 * g + h] = jnp.where(sub < 4, part, jnp.where(sub == 4, deep, 0.0))
                middle[2 * g + h] = jnp.where(sub < 3, mid, 0.0)
            here = lane == g
            return jnp.where(here, low, bounds[0]), jnp.where(here, high, bounds[1])

        start = group[0:8, :]
        return lax.fori_loop(0, group.shape[0] // 8, two_blocks, (start, start), unroll=8)

    row_low, row_high = prepare(row_group, rows, row_mid)
    col_low, col_high = prepare(col_group, cols, col_mid)

    firsts = jnp.broadcast_to(pairs[0:1, :], (8, BLK))
    seconds = jnp.broadcast_to(pairs[1:2, :], (8, BLK))

    def pick(bound, index):
        got = jnp.take_along_axis(bound, index >> 1, axis=1, mode="promise_in_bounds")
        return jnp.where((index & 1) == 1, pltpu.roll(got, 4, 0), got)

    xl, xh = pick(row_low, firsts), pick(row_high, firsts)
    yl, yh = pick(col_low, seconds), pick(col_high, seconds)
    apart = wrap(jnp.where(sub < 3, 0.5 * ((yl + yh) - (xl + xh)), 0.0))
    gap = jnp.abs(apart) - 0.5 * ((yh - yl) + (xh - xl))
    gap = jnp.where(sub < 3, jnp.maximum(gap, 0.0), 0.0)
    gap2 = jnp.sum(gap * gap, axis=0, keepdims=True)
    near_by = jnp.broadcast_to(gap2, (8, BLK)) < cutoff_sq + 0.01
    active = jnp.where(near_by & (lane.astype(f32) < tables[2]), 1.0, 0.0)
    big_sub = lax.broadcasted_iota(jnp.int32, (BLK, BLK), 0)
    big_lane = lax.broadcasted_iota(jnp.int32, (BLK, BLK), 1)
    across = (((1,), (1,)), ((), ()))
    down = (((1,), (0,)), ((), ()))

    def dot(u, v, dims):
        return lax.dot_general(u, v, dims, preferred_element_type=f32)

    upto = dot(jnp.where(big_lane <= big_sub, 1.0, 0.0).astype(bf16), active.astype(bf16), across)[:, 0:1]
    before = dot(jnp.where(big_lane < big_sub, 1.0, 0.0).astype(bf16), active.astype(bf16), across)[:, 0:1]
    place = big_lane.astype(f32)
    move = jnp.where((place >= before) & (place < upto), 1.0, 0.0).astype(bf16)
    both = jnp.where(sub == 0, firsts, seconds).astype(f32).astype(bf16)
    packed = dot(both, move, down)
    count = jnp.broadcast_to(jnp.sum(active, axis=1, keepdims=True), (8, BLK))
    spare = jnp.where(sub == 0, float(NA), float(NB))
    packed = jnp.where(lane.astype(f32) < count, packed, spare)
    listed[...] = jnp.where(sub == 2, count, packed).astype(jnp.int32)
    copy = pltpu.make_async_copy(listed, todo, sem)
    copy.start()
    copy.wait()
    total = todo[2, 0]
    row_id, col_id = lax.axis_index("row"), lax.axis_index("col")
    scale = 1.5 * cutoff_sq

    def force_sources(tile):
        well = tile[4:5]
        v = jnp.where(sub < 3, tile * well, jnp.where(sub == 3, well, 0.0))
        head, mid, low = split3(v)
        first = jnp.where(sub < 4, head, pltpu.roll(low, 4, 0))
        return jnp.concatenate([first, mid], axis=0).astype(bf16)

    def fold(v):
        v = v[0:8] + v[8:16]
        return v + pltpu.roll(v, 4, 0)

    def entry(p):
        valid = (p >= 0) & (p < total)
        q = jnp.clip(p, 0, BLK - 1)
        return jnp.where(valid, todo[0, q], NA), jnp.where(valid, todo[1, q], NB)

    def finish(n, p, vr, vc):
        a, b = entry(p)
        mine, theirs = rows[a], cols[b]
        shift = wrap(col_mid[b] - row_mid[a])
        vr, vc = fold(vr), fold(vc)
        fr = (vr + (shift - mine) * vr[3:4]) * mine[4:5]
        fc = (vc - (shift + theirs) * vc[3:4]) * theirs[4:5]
        same = (b // BPD == row_id) & (a == col_id * BPD + b % BPD)
        fc = fc * jnp.where(same, 0.0, 1.0)
        row_acc[a] = row_acc[a] + fr
        col_acc[b] = col_acc[b] + fc

    def pull(n, head, tail):
        px, py = sources[n, 0], sources[n, 1]
        return dot(py, head, across) + dot(py, tail, across), dot(px, head, down) + dot(px, tail, down)

    def coefficients(n, p, terms):
        for m in range(0, BLK, 16):
            w, soft, sig2 = [v[m : m + 16] for v in terms]
            w = jnp.maximum(w, 0.0)
            guess = pl.reciprocal(soft, approx=True)
            inv = guess * (2.0 - soft * guess)
            ratio = sig2 * inv
            u3 = ratio * ratio * ratio
            t = inv * w
            t1 = t + 1.0
            k = (t1 - u3 * (t1 + t)) * (u3 * w)
            high = k.astype(bf16)
            k_parts[n, 0, m : m + 16, :] = high
            k_parts[n, 1, m : m + 16, :] = (k - high.astype(f32)).astype(bf16)
        a, b = entry(p)
        sources[n, 0] = force_sources(rows[a])
        sources[n, 1] = force_sources(cols[b])

    def describe(n, p):
        a, b = entry(p)
        mine, theirs = rows[a], cols[b]
        other = theirs + wrap(col_mid[b] - row_mid[a])
        sq = mine * mine
        norm = (sq[0:1] + sq[1:2] + sq[2:3]) * (1.0 / cutoff_sq)
        left = jnp.where(sub < 5, mine, jnp.where(sub == 5, norm, jnp.where(sub == 6, sq[3:4], 1.0)))
        head, mid, low = split3(left)
        lefts[n] = jnp.concatenate([head, head, head, mid, mid, low], axis=0).T.astype(bf16)
        sq = other * other
        norm = sq[0:1] + sq[1:2] + sq[2:3]
        size2 = sq[3:4]
        inv_c = 1.0 / scale
        for_w = jnp.where(
            sub < 3, other * (2.0 / cutoff_sq),
            jnp.where(sub == 5, -1.0, jnp.where(sub == 7, 1.0 - norm * (1.0 / cutoff_sq), 0.0)),
        )
        for_sig = jnp.where(
            sub == 3, other * (2.0 * inv_c), jnp.where(sub == 6, inv_c, jnp.where(sub == 7, size2 * inv_c, 0.0))
        )
        for_soft = jnp.where(
            sub < 3, other * (-2.0 * inv_c),
            jnp.where(sub == 5, cutoff_sq * inv_c, jnp.where(sub == 7, (norm + size2) * inv_c, for_sig)),
        )
        for m, right in enumerate((for_w, for_soft, for_sig)):
            head, mid, low = split3(right)
            rights[n, m] = jnp.concatenate([head, mid, low, head, mid, head], axis=0).astype(bf16)

    def turn(g, carry):
        held = [(k_parts[n, 0], k_parts[n, 1]) for n in range(4)]
        terms = [[dot(lefts[n], rights[n, m], down) for m in range(3)] for n in range(4)]
        for n in range(4):
            finish(n, 4 * (g - 2) + n, *pull(n, *held[n]))
        for n in range(4):
            coefficients(n, 4 * (g - 1) + n, terms[n])
        for n in range(4):
            describe(n, 4 * g + n)
        return carry

    lax.fori_loop(0, (total + 4 - 1) // 4 + 2, turn, 0)
    on_row[...] = row_acc[0:NA, 0:4, :]
    on_col[...] = col_acc[0:NB, 0:4, :]


def scatter_kernel(
    on_row, on_col, row_share, col_share,
    far_in, far_out, core_in, near_out, near_in, near_sum, z_relay, z_in, y_in, zl_out, zl_in,
    send_sem, far_sem, core_sem, near_sem, z_sem, y_sem, zl_sem,
):
    me = Place()
    barrier = greet(me)
    pl.semaphore_wait(barrier, len(me.partners()))
    started = []

    def ship(src, dst, sem, device):
        copy = pltpu.make_async_remote_copy(
            src_ref=src, dst_ref=dst, send_sem=send_sem.at[len(started)], recv_sem=sem,
            device_id=device, device_id_type=MESH,
        )
        copy.start()
        started.append(copy)

    def arrived(dst, sem):
        pltpu.make_async_remote_copy(
            src_ref=dst, dst_ref=dst, send_sem=send_sem.at[0], recv_sem=sem,
            device_id=me.at_core(), device_id_type=MESH,
        ).wait_recv()

    def far(x, k, device):
        ship(on_col.at[me.z_far, x, k], far_in.at[me.x * NK + me.k], far_sem.at[me.x * NK + me.k], device)

    for x in me.x_mates:
        far(x, me.k, me.at_x(x))
        far(x, 1 - me.k, me.at_x_other(x))
    far(me.x, 1 - me.k, me.at_core())
    near = [(me.zh + 3) % NZH, me.zh, (me.zh + 1) % NZH]
    j_from, j_to = 2 * me.k, 2 - 2 * me.k
    for j, zh in enumerate(near):
        ship(on_col.at[zh, :, 1 - me.k], core_in.at[j], core_sem.at[j], me.at_core())
    for y in me.y_mates:
        ship(on_row.at[:, y], y_in.at[me.y], y_sem.at[me.y], me.at_y(y))
    for j, zh in enumerate(near):
        arrived(core_in.at[j], core_sem.at[j])
        for x in me.x_mates:
            near_out[x, j] = on_col[zh, x, me.k] + core_in[j, x]
        near_sum[j] = on_col[zh, me.x, me.k] + core_in[j, me.x]
    for x in me.x_mates:
        ship(near_out.at[x], near_in.at[me.x], near_sem.at[me.x], me.at_x(x))
    total = on_col[me.z_far, me.x, me.k]
    order = [(me.x, 1 - me.k)]
    for x in (me.x_mates[1], me.x_mates[2], me.x_mates[0]):
        order += [(x, me.k), (x, 1 - me.k)]
    for x, k in order:
        arrived(far_in.at[x * NK + k], far_sem.at[x * NK + k])
        total = total + far_in[x * NK + k]
    far_out[...] = total
    ship(far_out, z_in.at[0], z_sem.at[0], me.at_z(me.z_to))

    for x in (me.x_mates[1], me.x_mates[2], me.x_mates[0]):
        arrived(near_in.at[x], near_sem.at[x])
    near_sum[...] = (
        near_sum[...] + near_in[me.x_mates[0]] + near_in[me.x_mates[1]] + near_in[me.x_mates[2]]
    )
    ship(near_sum.at[j_from], z_in.at[1], z_sem.at[1], me.at_z(me.z_from))

    total = on_row[:, me.y]
    for y in me.y_mates:
        arrived(y_in.at[y], y_sem.at[y])
        total = total + y_in[y]
    zl_out[...] = total
    for zl in me.zl_mates:
        ship(zl_out.at[zl], zl_in.at[me.zl], zl_sem.at[me.zl], me.at_zl(zl))

    arrived(z_in.at[0], z_sem.at[0])
    z_relay[...] = z_in[0] + near_sum[j_to]
    ship(z_relay, z_in.at[2], z_sem.at[2], me.at_z(me.z_to))
    row_total, col_total = zl_out[me.zl], near_sum[1]
    for zl in me.zl_mates:
        arrived(zl_in.at[zl], zl_sem.at[zl])
        row_total = row_total + zl_in[zl]
    for e in range(BPD):
        row_share[:, BLK * e : BLK * (e + 1)] = row_total[e, 0:3]
    arrived(z_in.at[1], z_sem.at[1])
    col_total = col_total + z_in[1]
    arrived(z_in.at[2], z_sem.at[2])
    col_total = col_total + z_in[2]
    for e in range(BPD):
        col_share[:, BLK * e : BLK * (e + 1)] = col_total[e, 0:3]
    for copy in started:
        copy.wait_send()


def body(positions, velocities, old_forces, types, sigma_table, epsilon_table, pairs, live):
    f32 = jnp.float32
    dma = pltpu.SemaphoreType.DMA
    vmem = pl.BlockSpec(memory_space=VMEM)
    hbm = pl.BlockSpec(memory_space=pltpu.HBM)
    i32 = jnp.int32
    coords = positions.shape
    row_group, col_group, moved_near, pairs_near, tables = pl.pallas_call(
        gather_kernel,
        out_shape=(
            jax.ShapeDtypeStruct((NA * 4, BLK), f32),
            jax.ShapeDtypeStruct((NB * 4, BLK), f32),
            jax.ShapeDtypeStruct(coords, f32),
            jax.ShapeDtypeStruct((2, BLK), i32),
            jax.ShapeDtypeStruct((3, 8, BLK), f32),
        ),
        in_specs=[hbm] * 8,
        out_specs=(vmem,) * 5,
        scratch_shapes=[
            VMEM(coords, f32),
            VMEM(coords, f32),
            VMEM(coords, f32),
            VMEM((BPD, BLK), i32),
            pltpu.SMEM(sigma_table.shape, f32),
            pltpu.SMEM(epsilon_table.shape, f32),
            pltpu.SMEM((1, 1), i32),
            VMEM((4 * BPD, BLK), f32),
            dma((8,)),
            dma((48,)),
            dma((COLS,)),
            dma((ROWS,)),
        ],
        compiler_params=pltpu.CompilerParams(collective_id=0, has_side_effects=True, vmem_limit_bytes=8 << 20),
        name="gather",
    )(
        *[
            pltpu.with_memory_space_constraint(v, pltpu.HBM)
            for v in (
                positions, velocities, old_forces, types.reshape(BPD, BLK), sigma_table, epsilon_table,
                pairs.reshape(2, BLK),
            )
        ],
        live,
    )

    def pair_call(*refs):
        return pair_kernel(ROWS * cell_side, COLS * cell_side, *refs)

    on_row, on_col, moved = pl.pallas_call(
        pair_call,
        out_shape=(
            jax.ShapeDtypeStruct((NA, 4, BLK), f32),
            jax.ShapeDtypeStruct((NB, 4, BLK), f32),
            jax.ShapeDtypeStruct(positions.shape, f32),
        ),
        in_specs=[vmem] * 5,
        out_specs=(vmem, vmem, vmem),
        scratch_shapes=[
            VMEM((NA + 1, 8, BLK), f32),
            VMEM((NB + 1, 8, BLK), f32),
            VMEM((NA + 1, 8, BLK), f32),
            VMEM((NB + 1, 8, BLK), f32),
            VMEM((NA + 1, 8, BLK), f32),
            VMEM((NB + 1, 8, BLK), f32),
            VMEM((8, BLK), jnp.int32),
            pltpu.SMEM((8, BLK), jnp.int32),
            VMEM((4, 2, BLK, BLK), jnp.bfloat16),
            VMEM((4, BLK, 48), jnp.bfloat16),
            VMEM((4, 3, 48, BLK), jnp.bfloat16),
            VMEM((4, 2, 16, BLK), jnp.bfloat16),
            dma,
        ],
        compiler_params=pltpu.CompilerParams(vmem_limit_bytes=16 << 20),
        name="pairs",
    )(
        pairs_near, tables, row_group, col_group, moved_near,
    )

    tile = (BPD, 4, BLK)
    row_share, col_share = pl.pallas_call(
        scatter_kernel,
        out_shape=(jax.ShapeDtypeStruct(positions.shape, f32), jax.ShapeDtypeStruct(positions.shape, f32)),
        in_specs=[vmem] * 2,
        out_specs=(vmem, vmem),
        scratch_shapes=[
            VMEM((NX * NK,) + tile, f32),
            VMEM(tile, f32),
            VMEM((3, NX) + tile, f32),
            VMEM((NX, 3) + tile, f32),
            VMEM((NX, 3) + tile, f32),
            VMEM((3,) + tile, f32),
            VMEM(tile, f32),
            VMEM((3,) + tile, f32),
            VMEM((NY, NZL) + tile, f32),
            VMEM((NZL,) + tile, f32),
            VMEM((NZL,) + tile, f32),
            dma((24,)),
            dma((NX * NK,)),
            dma((3,)),
            dma((NX,)),
            dma((3,)),
            dma((NY,)),
            dma((NZL,)),
        ],
        compiler_params=pltpu.CompilerParams(collective_id=1, has_side_effects=True, vmem_limit_bytes=8 << 20),
        name="scatter",
    )(
        on_row.reshape((NZL, NY) + tile),
        on_col.reshape((NZH, NX, NK) + tile),
    )
    new_forces = row_share + col_share
    new_velocities = velocities + 0.5 * time_step * (old_forces + new_forces)
    return moved, new_velocities, new_forces


def solution(mesh):
    in_specs = (
        P(None, ("row", "col")),
        P(None, ("row", "col")),
        P(None, ("row", "col")),
        P(("row", "col")),
        P(),
        P(),
        P("row", "col", None, None),
        P("row", "col"),
    )
    out_specs = (P(None, ("row", "col")), P(None, ("row", "col")), P(None, ("row", "col")))
    return jax.shard_map(body, mesh=mesh, in_specs=in_specs, out_specs=out_specs, check_vma=False)
```

```python
import math

import jax
import jax.numpy as jnp
from jax import lax
from jax.experimental import pallas as pl
from jax.experimental.pallas import tpu as pltpu
from jax.sharding import PartitionSpec as P

BLK = 128
BPD = 4
NZH, NX, NK = 4, 4, 2
NZL, NY = 4, 4
ROWS, COLS = NZH * NX * NK, NZL * NY
NA, NB = COLS * BPD, ROWS * BPD

time_step = 0.05
cell_side = 5.3
cutoff_sq = 6.25

MESH = pl.DeviceIdType.MESH
VMEM = pltpu.VMEM


class Place:
    def __init__(self):
        r, c = lax.axis_index("row"), lax.axis_index("col")
        self.r, self.c = r, c
        self.zh, self.x, self.k = r // (NX * NK), (r // NK) % NX, r % NK
        self.zl, self.y = c // NY, c % NY
        self.z_from = (self.zh + 3 - 2 * self.k) % NZH
        self.z_to = (self.zh + 1 + 2 * self.k) % NZH
        self.z_far = (self.zh + 2) % NZH
        self.x_mates = [(self.x + s) % NX for s in (2, 1, 3)]
        self.zl_mates = [(self.zl + s) % NZL for s in (2, 1, 3)]
        self.y_mates = [(self.y + s) % NY for s in (2, 1, 3)]

    def row_slot(self, zh, x, k):
        return (zh * NX + x) * NK + k

    def col_slot(self, zl, y):
        return zl * NY + y

    def at_z(self, zh):
        return (self.row_slot(zh, self.x, self.k), self.c)

    def at_x(self, x):
        return (self.row_slot(self.zh, x, self.k), self.c)

    def at_x_other(self, x):
        return (self.row_slot(self.zh, x, 1 - self.k), self.c)

    def at_core(self):
        return (self.row_slot(self.zh, self.x, 1 - self.k), self.c)

    def at_zl(self, zl):
        return (self.r, self.col_slot(zl, self.y))

    def at_y(self, y):
        return (self.r, self.col_slot(self.zl, y))

    def partners(self):
        return (
            [self.at_z(self.z_from), self.at_z(self.z_to), self.at_core()]
            + [self.at_x(x) for x in self.x_mates]
            + [self.at_x_other(x) for x in self.x_mates]
            + [self.at_zl(z) for z in self.zl_mates]
            + [self.at_y(y) for y in self.y_mates]
        )


def greet(me):
    barrier = pltpu.get_barrier_semaphore()
    for device in me.partners():
        pl.semaphore_signal(barrier, inc=1, device_id=device, device_id_type=MESH)
    return barrier


def gather_kernel(
    pos_hbm, vel_hbm, old_hbm, kind_hbm, sigma_hbm, epsilon_hbm, pairs_hbm, live_hbm,
    row_group, col_group, moved, pairs, tables, row_mid, col_mid, row_ends, col_ends,
    pos, vel, old, kind, sigma, epsilon, live, mine, local_sem, send_sem, row_sem, col_sem,
):
    me = Place()
    barrier = greet(me)
    local = [
        pltpu.make_async_copy(src, dst, local_sem.at[n])
        for n, (src, dst) in enumerate(
            (
                (pos_hbm, pos), (vel_hbm, vel), (old_hbm, old), (kind_hbm, kind),
                (sigma_hbm, sigma), (epsilon_hbm, epsilon), (live_hbm, live), (pairs_hbm, pairs),
            )
        )
    ]
    for copy in local:
        copy.start()
    for copy in local[:4]:
        copy.wait()
    moved[...] = pos[...] + time_step * vel[...] + 0.5 * time_step * time_step * old[...]
    kinds = kind[...].astype(jnp.float32)
    for e in range(BPD):
        mine[4 * e : 4 * e + 3, :] = moved[:, BLK * e : BLK * (e + 1)]
        mine[4 * e + 3 : 4 * e + 4, :] = kinds[e : e + 1, :]
    packet = mine[...]
    row_group[pl.ds(pl.multiple_of(me.c * 16, 16), 16), :] = packet
    col_group[pl.ds(pl.multiple_of(me.r * 16, 16), 16), :] = packet
    pl.semaphore_wait(barrier, len(me.partners()))

    started = []

    def ship(src, group, sems, slot, device):
        copy = pltpu.make_async_remote_copy(
            src_ref=src,
            dst_ref=group.at[pl.ds(pl.multiple_of(slot * 16, 16), 16), :],
            send_sem=send_sem.at[len(started)],
            recv_sem=sems.at[slot],
            device_id=device,
            device_id_type=MESH,
        )
        copy.start()
        started.append(copy)

    def arrived(group, sems, slot):
        view = group.at[pl.ds(pl.multiple_of(slot * 16, 16), 16), :]
        pltpu.make_async_remote_copy(
            src_ref=view,
            dst_ref=view,
            send_sem=send_sem.at[0],
            recv_sem=sems.at[slot],
            device_id=me.at_core(),
            device_id_type=MESH,
        ).wait_recv()
        return view

    own_row = me.row_slot(me.zh, me.x, me.k)
    for zh in (me.z_to, me.z_from):
        ship(mine, col_group, col_sem, own_row, me.at_z(zh))
    for zl in me.zl_mates:
        ship(mine, row_group, row_sem, me.c, me.at_zl(zl))
    for x in me.x_mates:
        ship(mine, col_group, col_sem, own_row, me.at_x(x))
    for y in me.y_mates:
        ship(mine, row_group, row_sem, me.c, me.at_y(y))
    ship(mine, col_group, col_sem, own_row, me.at_core())

    for copy in local[4:]:
        copy.wait()
    lane = lax.broadcasted_iota(jnp.int32, (8, BLK), 1)
    sizes = jnp.zeros((8, BLK), jnp.float32)
    wells = jnp.zeros((8, BLK), jnp.float32)
    for n in range(sigma.shape[0]):
        sizes = jnp.where(lane == n, 0.5 * sigma[n], sizes)
        wells = jnp.where(lane == n, epsilon[n], wells)
    tables[0] = sizes
    tables[1] = math.sqrt(16.0 / cutoff_sq) * jnp.sqrt(wells)
    tables[2] = jnp.full((8, BLK), live[0, 0].astype(jnp.float32))

    def spread(zh, relay=False, last=False):
        slot = me.row_slot(zh, me.x, me.k)
        view = arrived(col_group, col_sem, slot)
        if relay:
            ship(view, col_group, col_sem, slot, me.at_z(me.z_to))
        for x in me.x_mates:
            ship(view, col_group, col_sem, slot, me.at_x(x))
            if last:
                ship(view, col_group, col_sem, slot, me.at_x_other(x))
        ship(view, col_group, col_sem, slot, me.at_core())

    def share(zh, x):
        slot = me.row_slot(zh, x, me.k)
        view = arrived(col_group, col_sem, slot)
        ship(view, col_group, col_sem, slot, me.at_core())

    def fan_out(zl):
        slot = me.col_slot(zl, me.y)
        view = arrived(row_group, row_sem, slot)
        for y in me.y_mates:
            ship(view, row_group, row_sem, slot, me.at_y(y))

    def bound(group, middle, ends, slots):
        found = []
        for slot in slots:
            for h in range(2):
                both = group[pl.ds(pl.multiple_of(slot * 16 + 8 * h, 8), 8), :]
                low = jnp.broadcast_to(jnp.min(both, axis=1, keepdims=True), (8, BLK))
                high = jnp.broadcast_to(jnp.max(both, axis=1, keepdims=True), (8, BLK))
                middle[2 * slot + h] = 0.5 * (low + high)
                found.append((lane == 2 * slot + h, low, high))
        lows, highs = ends[0], ends[1]
        for here, low, high in found:
            lows = jnp.where(here, low, lows)
            highs = jnp.where(here, high, highs)
        ends[0], ends[1] = lows, highs

    def bound_rows(slots):
        bound(row_group, row_mid, row_ends, slots)

    def bound_cols(slots):
        bound(col_group, col_mid, col_ends, slots)

    def take_rows(slots):
        for slot in slots:
            arrived(row_group, row_sem, slot)
        bound_rows(slots)

    def take_cols(slots):
        for slot in slots:
            arrived(col_group, col_sem, slot)
        bound_cols(slots)

    for ends in (row_ends, col_ends):
        ends[...] = jnp.zeros_like(ends)
    bound_rows([me.c])
    bound_cols([own_row])
    for zl in me.zl_mates[1:]:
        fan_out(zl)
    for x in me.x_mates:
        share(me.zh, x)
    fan_out(me.zl_mates[0])
    bound_rows([me.col_slot(zl, me.y) for zl in me.zl_mates])
    bound_cols([me.row_slot(me.zh, x, me.k) for x in me.x_mates])
    spread(me.z_from, relay=True)
    spread(me.z_to)
    ends_z = (me.z_from, me.z_to)
    bound_cols([me.row_slot(zh, me.x, me.k) for zh in ends_z])
    xs = [me.x] + me.x_mates
    take_cols([me.row_slot(me.zh, x, 1 - me.k) for x in xs])
    take_rows([me.col_slot(me.zl, y) for y in me.y_mates])
    for x in me.x_mates:
        share(me.z_from, x)
        share(me.z_to, x)
    bound_cols([me.row_slot(zh, x, me.k) for x in me.x_mates for zh in ends_z])
    take_rows([me.col_slot(zl, y) for zl in me.zl_mates for y in me.y_mates])
    spread(me.z_far, last=True)
    take_cols([me.row_slot(zh, x, 1 - me.k) for x in xs for zh in ends_z])
    bound_cols([me.row_slot(me.z_far, me.x, me.k)])
    take_cols([me.row_slot(me.z_far, me.x, 1 - me.k)])
    take_cols([me.row_slot(me.z_far, x, k) for x in me.x_mates for k in (me.k, 1 - me.k)])
    for copy in started:
        copy.wait_send()


def split3(v):
    head = v.astype(jnp.bfloat16).astype(jnp.float32)
    rest = v - head
    mid = rest.astype(jnp.bfloat16).astype(jnp.float32)
    return head, mid, rest - mid


def pair_kernel(
    box_y, box_z, pairs, tables, row_group, col_group, row_mid, col_mid, row_ends, col_ends, moved_in,
    on_row, on_col, moved, rows, cols, row_acc, col_acc, listed, todo, k_parts, lefts, rights, sources, shifts, sem,
):
    f32, bf16 = jnp.float32, jnp.bfloat16
    moved[...] = moved_in[...]
    row_acc[...] = jnp.zeros_like(row_acc)
    col_acc[...] = jnp.zeros_like(col_acc)
    sub = lax.broadcasted_iota(jnp.int32, (8, BLK), 0)
    lane = lax.broadcasted_iota(jnp.int32, (8, BLK), 1)
    sizes, wells = tables[0], tables[1]
    kind_row = (sub == 3) | (sub == 7)
    box = jnp.where(sub == 0, BPD * cell_side, jnp.where(sub == 1, box_y, jnp.where(sub == 2, box_z, 1.0)))
    inverse_box = 1.0 / box

    def wrap(v):
        return v - box * jnp.floor(v * inverse_box + 0.5)

    def look_up(group, middle, index):
        g = index // 2
        mid = middle[g]
        both = group[pl.ds(pl.multiple_of(8 * g, 8), 8), :]
        odd = jnp.full((8, BLK), index % 2) == 1
        near = jnp.where(kind_row, both, both - mid)
        near = jnp.where(odd, pltpu.roll(near, 4, 0), near)
        mid = jnp.where(sub < 3, jnp.where(odd, pltpu.roll(mid, 4, 0), mid), 0.0)
        kinds = jnp.broadcast_to(near[3:4], (8, BLK)).astype(jnp.int32)
        size = jnp.take_along_axis(sizes, kinds, axis=1, mode="promise_in_bounds")
        well = jnp.take_along_axis(wells, kinds, axis=1, mode="promise_in_bounds")
        tile = jnp.where(sub < 3, near, jnp.where(sub == 3, size, jnp.where(sub == 4, well, 0.0)))
        return tile, mid

    firsts = jnp.broadcast_to(pairs[0:1, :], (8, BLK))
    seconds = jnp.broadcast_to(pairs[1:2, :], (8, BLK))

    def pick(bound, index):
        got = jnp.take_along_axis(bound, index >> 1, axis=1, mode="promise_in_bounds")
        return jnp.where((index & 1) == 1, pltpu.roll(got, 4, 0), got)

    xl, xh = pick(row_ends[0], firsts), pick(row_ends[1], firsts)
    yl, yh = pick(col_ends[0], seconds), pick(col_ends[1], seconds)
    apart = wrap(jnp.where(sub < 3, 0.5 * ((yl + yh) - (xl + xh)), 0.0))
    gap = jnp.abs(apart) - 0.5 * ((yh - yl) + (xh - xl))
    gap = jnp.where(sub < 3, jnp.maximum(gap, 0.0), 0.0)
    gap2 = jnp.sum(gap * gap, axis=0, keepdims=True)
    near_by = jnp.broadcast_to(gap2, (8, BLK)) < cutoff_sq + 0.01
    active = jnp.where(near_by & (lane.astype(f32) < tables[2]), 1.0, 0.0)
    big_sub = lax.broadcasted_iota(jnp.int32, (BLK, BLK), 0)
    big_lane = lax.broadcasted_iota(jnp.int32, (BLK, BLK), 1)
    across = (((1,), (1,)), ((), ()))
    down = (((1,), (0,)), ((), ()))

    def dot(u, v, dims):
        return lax.dot_general(u, v, dims, preferred_element_type=f32)

    upto = dot(jnp.where(big_lane <= big_sub, 1.0, 0.0).astype(bf16), active.astype(bf16), across)[:, 0:1]
    before = dot(jnp.where(big_lane < big_sub, 1.0, 0.0).astype(bf16), active.astype(bf16), across)[:, 0:1]
    place = big_lane.astype(f32)
    move = jnp.where((place >= before) & (place < upto), 1.0, 0.0).astype(bf16)
    both = jnp.where(sub == 0, firsts, seconds).astype(f32).astype(bf16)
    packed = dot(both, move, down)
    count = jnp.broadcast_to(jnp.sum(active, axis=1, keepdims=True), (8, BLK))
    spare = jnp.where(sub == 0, float(NA), float(NB))
    packed = jnp.where(lane.astype(f32) < count, packed, spare)
    listed[...] = jnp.where(sub == 2, count, packed).astype(jnp.int32)
    copy = pltpu.make_async_copy(listed, todo, sem)
    copy.start()
    copy.wait()
    total = todo[2, 0]
    row_id, col_id = lax.axis_index("row"), lax.axis_index("col")
    scale = 1.5 * cutoff_sq

    def force_sources(tile):
        well = tile[4:5]
        v = jnp.where(sub < 3, tile * well, jnp.where(sub == 3, well, 0.0))
        head, mid, low = split3(v)
        first = jnp.where(sub < 4, head, pltpu.roll(low, 4, 0))
        return jnp.concatenate([first, mid], axis=0).astype(bf16)

    def fold(v):
        v = v[0:8] + v[8:16]
        return v + pltpu.roll(v, 4, 0)

    def entry(p):
        valid = (p >= 0) & (p < total)
        q = jnp.clip(p, 0, BLK - 1)
        return jnp.where(valid, todo[0, q], NA), jnp.where(valid, todo[1, q], NB)

    def finish(n, p, vr, vc):
        a, b = entry(p)
        mine, theirs = rows[a], cols[b]
        shift = shifts[p + 4]
        vr, vc = fold(vr), fold(vc)
        fr = (vr + (shift - mine) * vr[3:4]) * mine[4:5]
        fc = (vc - (shift + theirs) * vc[3:4]) * theirs[4:5]
        same = (b // BPD == row_id) & (a == col_id * BPD + b % BPD)
        fc = fc * jnp.where(same, 0.0, 1.0)
        row_acc[a] = row_acc[a] + fr
        col_acc[b] = col_acc[b] + fc

    def pull(n, head, tail):
        px, py = sources[n, 0], sources[n, 1]
        px, py = jnp.concatenate([px, px], axis=1), jnp.concatenate([py, py], axis=1)
        return (
            dot(py, jnp.concatenate([head, tail], axis=1), across),
            dot(px, jnp.concatenate([head, tail], axis=0), down),
        )

    def coefficients(n, p, terms):
        for m in range(0, BLK, 16):
            w, soft, sig2 = [terms[m : m + 16, BLK * v : BLK * (v + 1)] for v in range(3)]
            w = jnp.maximum(w, 0.0)
            guess = pl.reciprocal(soft, approx=True)
            inv = guess * (2.0 - soft * guess)
            ratio = sig2 * inv
            u3 = ratio * ratio * ratio
            t = inv * w
            t1 = t + 1.0
            k = (t1 - u3 * (t1 + t)) * (u3 * w)
            high = k.astype(bf16)
            k_parts[n, 0, m : m + 16, :] = high
            k_parts[n, 1, m : m + 16, :] = (k - high.astype(f32)).astype(bf16)
        a, b = entry(p)
        sources[n, 0] = force_sources(rows[a])
        sources[n, 1] = force_sources(cols[b])

    def describe(n, p):
        a, b = entry(p)
        mine, near_mid = look_up(row_group, row_mid, jnp.minimum(a, NA - 1))
        theirs, far_mid = look_up(col_group, col_mid, jnp.minimum(b, NB - 1))
        rows[a] = mine
        cols[b] = theirs
        shift = wrap(far_mid - near_mid)
        shifts[p + 4] = shift
        other = theirs + shift
        sq = mine * mine
        norm = (sq[0:1] + sq[1:2] + sq[2:3]) * (1.0 / cutoff_sq)
        left = jnp.where(sub < 5, mine, jnp.where(sub == 5, norm, jnp.where(sub == 6, sq[3:4], 1.0)))
        head, mid, low = split3(left)
        lefts[n] = jnp.concatenate([head, head, head, mid, mid, low], axis=0).T.astype(bf16)
        sq = other * other
        norm = sq[0:1] + sq[1:2] + sq[2:3]
        size2 = sq[3:4]
        inv_c = 1.0 / scale
        for_w = jnp.where(
            sub < 3, other * (2.0 / cutoff_sq),
            jnp.where(sub == 5, -1.0, jnp.where(sub == 7, 1.0 - norm * (1.0 / cutoff_sq), 0.0)),
        )
        for_sig = jnp.where(
            sub == 3, other * (2.0 * inv_c), jnp.where(sub == 6, inv_c, jnp.where(sub == 7, size2 * inv_c, 0.0))
        )
        for_soft = jnp.where(
            sub < 3, other * (-2.0 * inv_c),
            jnp.where(sub == 5, cutoff_sq * inv_c, jnp.where(sub == 7, (norm + size2) * inv_c, for_sig)),
        )
        for m, right in enumerate((for_w, for_soft, for_sig)):
            head, mid, low = split3(right)
            rights[n, :, BLK * m : BLK * (m + 1)] = jnp.concatenate([head, mid, low, head, mid, head], axis=0).astype(bf16)

    def turn(g, carry):
        held = [(k_parts[n, 0], k_parts[n, 1]) for n in range(4)]
        terms = [dot(lefts[n], rights[n], down) for n in range(4)]
        for n in range(4):
            finish(n, 4 * (g - 1) + n, *pull(n, *held[n]))
        for n in range(4):
            coefficients(n, 4 * g + n, terms[n])
        for n in range(4):
            describe(n, 4 * (g + 1) + n)
        return carry

    groups = (total + 3) // 4
    for n in range(4):
        describe(n, n)
    lax.fori_loop(0, groups, turn, 0)
    for n in range(4):
        finish(n, 4 * (groups - 1) + n, *pull(n, k_parts[n, 0], k_parts[n, 1]))
    on_row[...] = row_acc[0:NA, 0:4, :]
    on_col[...] = col_acc[0:NB, 0:4, :]


def scatter_kernel(
    on_row, on_col, row_share, col_share,
    far_in, far_out, core_in, near_out, near_in, near_sum, z_relay, z_in, y_in, zl_out, zl_in,
    send_sem, far_sem, core_sem, near_sem, z_sem, y_sem, zl_sem,
):
    me = Place()
    barrier = greet(me)
    pl.semaphore_wait(barrier, len(me.partners()))
    started = []

    def ship(src, dst, sem, device):
        copy = pltpu.make_async_remote_copy(
            src_ref=src, dst_ref=dst, send_sem=send_sem.at[len(started)], recv_sem=sem,
            device_id=device, device_id_type=MESH,
        )
        copy.start()
        started.append(copy)

    def arrived(dst, sem):
        pltpu.make_async_remote_copy(
            src_ref=dst, dst_ref=dst, send_sem=send_sem.at[0], recv_sem=sem,
            device_id=me.at_core(), device_id_type=MESH,
        ).wait_recv()

    def far(x, k, device):
        ship(on_col.at[me.z_far, x, k], far_in.at[me.x * NK + me.k], far_sem.at[me.x * NK + me.k], device)

    for x in me.x_mates:
        far(x, me.k, me.at_x(x))
        far(x, 1 - me.k, me.at_x_other(x))
    far(me.x, 1 - me.k, me.at_core())
    near = [(me.zh + 3) % NZH, me.zh, (me.zh + 1) % NZH]
    j_from, j_to = 2 * me.k, 2 - 2 * me.k
    for j, zh in enumerate(near):
        ship(on_col.at[zh, :, 1 - me.k], core_in.at[j], core_sem.at[j], me.at_core())
    for y in me.y_mates:
        ship(on_row.at[:, y], y_in.at[me.y], y_sem.at[me.y], me.at_y(y))
    for j, zh in enumerate(near):
        arrived(core_in.at[j], core_sem.at[j])
        for x in me.x_mates:
            near_out[x, j] = on_col[zh, x, me.k] + core_in[j, x]
        near_sum[j] = on_col[zh, me.x, me.k] + core_in[j, me.x]
    for x in me.x_mates:
        ship(near_out.at[x], near_in.at[me.x], near_sem.at[me.x], me.at_x(x))
    total = on_col[me.z_far, me.x, me.k]
    order = [(me.x, 1 - me.k)]
    for x in (me.x_mates[1], me.x_mates[2], me.x_mates[0]):
        order += [(x, me.k), (x, 1 - me.k)]
    for x, k in order:
        arrived(far_in.at[x * NK + k], far_sem.at[x * NK + k])
        total = total + far_in[x * NK + k]
    far_out[...] = total
    ship(far_out, z_in.at[0], z_sem.at[0], me.at_z(me.z_to))

    for x in (me.x_mates[1], me.x_mates[2], me.x_mates[0]):
        arrived(near_in.at[x], near_sem.at[x])
    near_sum[...] = (
        near_sum[...] + near_in[me.x_mates[0]] + near_in[me.x_mates[1]] + near_in[me.x_mates[2]]
    )
    ship(near_sum.at[j_from], z_in.at[1], z_sem.at[1], me.at_z(me.z_from))

    total = on_row[:, me.y]
    for y in me.y_mates:
        arrived(y_in.at[y], y_sem.at[y])
        total = total + y_in[y]
    zl_out[...] = total
    for zl in me.zl_mates:
        ship(zl_out.at[zl], zl_in.at[me.zl], zl_sem.at[me.zl], me.at_zl(zl))

    arrived(z_in.at[0], z_sem.at[0])
    z_relay[...] = z_in[0] + near_sum[j_to]
    ship(z_relay, z_in.at[2], z_sem.at[2], me.at_z(me.z_to))
    row_total, col_total = zl_out[me.zl], near_sum[1]
    for zl in me.zl_mates:
        arrived(zl_in.at[zl], zl_sem.at[zl])
        row_total = row_total + zl_in[zl]
    for e in range(BPD):
        row_share[:, BLK * e : BLK * (e + 1)] = row_total[e, 0:3]
    arrived(z_in.at[1], z_sem.at[1])
    col_total = col_total + z_in[1]
    arrived(z_in.at[2], z_sem.at[2])
    col_total = col_total + z_in[2]
    for e in range(BPD):
        col_share[:, BLK * e : BLK * (e + 1)] = col_total[e, 0:3]
    for copy in started:
        copy.wait_send()


def body(positions, velocities, old_forces, types, sigma_table, epsilon_table, pairs, live):
    f32 = jnp.float32
    dma = pltpu.SemaphoreType.DMA
    vmem = pl.BlockSpec(memory_space=VMEM)
    hbm = pl.BlockSpec(memory_space=pltpu.HBM)
    i32 = jnp.int32
    coords = positions.shape
    row_group, col_group, moved_near, pairs_near, tables, *boxes = pl.pallas_call(
        gather_kernel,
        out_shape=(
            jax.ShapeDtypeStruct((NA * 4, BLK), f32),
            jax.ShapeDtypeStruct((NB * 4, BLK), f32),
            jax.ShapeDtypeStruct(coords, f32),
            jax.ShapeDtypeStruct((2, BLK), i32),
            jax.ShapeDtypeStruct((3, 8, BLK), f32),
            jax.ShapeDtypeStruct((NA // 2, 8, BLK), f32),
            jax.ShapeDtypeStruct((NB // 2, 8, BLK), f32),
            jax.ShapeDtypeStruct((2, 8, BLK), f32),
            jax.ShapeDtypeStruct((2, 8, BLK), f32),
        ),
        in_specs=[hbm] * 8,
        out_specs=(vmem,) * 9,
        scratch_shapes=[
            VMEM(coords, f32),
            VMEM(coords, f32),
            VMEM(coords, f32),
            VMEM((BPD, BLK), i32),
            pltpu.SMEM(sigma_table.shape, f32),
            pltpu.SMEM(epsilon_table.shape, f32),
            pltpu.SMEM((1, 1), i32),
            VMEM((4 * BPD, BLK), f32),
            dma((8,)),
            dma((48,)),
            dma((COLS,)),
            dma((ROWS,)),
        ],
        compiler_params=pltpu.CompilerParams(collective_id=0, has_side_effects=True, vmem_limit_bytes=8 << 20),
        name="gather",
    )(
        *[
            pltpu.with_memory_space_constraint(v, pltpu.HBM)
            for v in (
                positions, velocities, old_forces, types.reshape(BPD, BLK), sigma_table, epsilon_table,
                pairs.reshape(2, BLK),
            )
        ],
        live,
    )

    def pair_call(*refs):
        return pair_kernel(ROWS * cell_side, COLS * cell_side, *refs)

    on_row, on_col, moved = pl.pallas_call(
        pair_call,
        out_shape=(
            jax.ShapeDtypeStruct((NA, 4, BLK), f32),
            jax.ShapeDtypeStruct((NB, 4, BLK), f32),
            jax.ShapeDtypeStruct(positions.shape, f32),
        ),
        in_specs=[vmem] * 9,
        out_specs=(vmem, vmem, vmem),
        scratch_shapes=[
            VMEM((NA + 1, 8, BLK), f32),
            VMEM((NB + 1, 8, BLK), f32),
            VMEM((NA + 1, 8, BLK), f32),
            VMEM((NB + 1, 8, BLK), f32),
            VMEM((8, BLK), jnp.int32),
            pltpu.SMEM((8, BLK), jnp.int32),
            VMEM((4, 2, BLK, BLK), jnp.bfloat16),
            VMEM((4, BLK, 48), jnp.bfloat16),
            VMEM((4, 48, 3 * BLK), jnp.bfloat16),
            VMEM((4, 2, 16, BLK), jnp.bfloat16),
            VMEM((BLK + 12, 8, BLK), f32),
            dma,
        ],
        compiler_params=pltpu.CompilerParams(vmem_limit_bytes=16 << 20),
        name="pairs",
    )(
        pairs_near, tables, row_group, col_group, *boxes, moved_near,
    )

    tile = (BPD, 4, BLK)
    row_share, col_share = pl.pallas_call(
        scatter_kernel,
        out_shape=(jax.ShapeDtypeStruct(positions.shape, f32), jax.ShapeDtypeStruct(positions.shape, f32)),
        in_specs=[vmem] * 2,
        out_specs=(vmem, vmem),
        scratch_shapes=[
            VMEM((NX * NK,) + tile, f32),
            VMEM(tile, f32),
            VMEM((3, NX) + tile, f32),
            VMEM((NX, 3) + tile, f32),
            VMEM((NX, 3) + tile, f32),
            VMEM((3,) + tile, f32),
            VMEM(tile, f32),
            VMEM((3,) + tile, f32),
            VMEM((NY, NZL) + tile, f32),
            VMEM((NZL,) + tile, f32),
            VMEM((NZL,) + tile, f32),
            dma((24,)),
            dma((NX * NK,)),
            dma((3,)),
            dma((NX,)),
            dma((3,)),
            dma((NY,)),
            dma((NZL,)),
        ],
        compiler_params=pltpu.CompilerParams(collective_id=1, has_side_effects=True, vmem_limit_bytes=8 << 20),
        name="scatter",
    )(
        on_row.reshape((NZL, NY) + tile),
        on_col.reshape((NZH, NX, NK) + tile),
    )
    new_forces = row_share + col_share
    new_velocities = velocities + 0.5 * time_step * (old_forces + new_forces)
    return moved, new_velocities, new_forces


def solution(mesh):
    in_specs = (
        P(None, ("row", "col")),
        P(None, ("row", "col")),
        P(None, ("row", "col")),
        P(("row", "col")),
        P(),
        P(),
        P("row", "col", None, None),
        P("row", "col"),
    )
    out_specs = (P(None, ("row", "col")), P(None, ("row", "col")), P(None, ("row", "col")))
    return jax.shard_map(body, mesh=mesh, in_specs=in_specs, out_specs=out_specs, check_vma=False)
```

```python
import math

import jax
import jax.numpy as jnp
from jax import lax
from jax.experimental import pallas as pl
from jax.experimental.pallas import tpu as pltpu
from jax.sharding import PartitionSpec as P

BLK = 128
BPD = 4
NZH, NX, NK = 4, 4, 2
NZL, NY = 4, 4
ROWS, COLS = NZH * NX * NK, NZL * NY
NA, NB = COLS * BPD, ROWS * BPD

time_step = 0.05
cell_side = 5.3
cutoff_sq = 6.25

MESH = pl.DeviceIdType.MESH
VMEM = pltpu.VMEM


class Place:
    def __init__(self):
        r, c = lax.axis_index("row"), lax.axis_index("col")
        self.r, self.c = r, c
        self.zh, self.x, self.k = r // (NX * NK), (r // NK) % NX, r % NK
        self.zl, self.y = c // NY, c % NY
        self.z_from = (self.zh + 3 - 2 * self.k) % NZH
        self.z_to = (self.zh + 1 + 2 * self.k) % NZH
        self.z_far = (self.zh + 2) % NZH
        self.x_mates = [(self.x + s) % NX for s in (2, 1, 3)]
        self.zl_mates = [(self.zl + s) % NZL for s in (2, 1, 3)]
        self.y_mates = [(self.y + s) % NY for s in (2, 1, 3)]

    def row_slot(self, zh, x, k):
        return (zh * NX + x) * NK + k

    def col_slot(self, zl, y):
        return zl * NY + y

    def at_z(self, zh):
        return (self.row_slot(zh, self.x, self.k), self.c)

    def at_x(self, x):
        return (self.row_slot(self.zh, x, self.k), self.c)

    def at_x_other(self, x):
        return (self.row_slot(self.zh, x, 1 - self.k), self.c)

    def at_core(self):
        return (self.row_slot(self.zh, self.x, 1 - self.k), self.c)

    def at_zl(self, zl):
        return (self.r, self.col_slot(zl, self.y))

    def at_y(self, y):
        return (self.r, self.col_slot(self.zl, y))

    def partners(self):
        return (
            [self.at_z(self.z_from), self.at_z(self.z_to), self.at_core()]
            + [self.at_x(x) for x in self.x_mates]
            + [self.at_x_other(x) for x in self.x_mates]
            + [self.at_zl(z) for z in self.zl_mates]
            + [self.at_y(y) for y in self.y_mates]
        )


def greet(me):
    barrier = pltpu.get_barrier_semaphore()
    for device in me.partners():
        pl.semaphore_signal(barrier, inc=1, device_id=device, device_id_type=MESH)
    return barrier


def gather_kernel(
    pos_hbm, vel_hbm, old_hbm, kind_hbm, sigma_hbm, epsilon_hbm, pairs_hbm,
    row_group, col_group, moved, pairs, tables, row_mid, col_mid, row_ends, col_ends,
    pos, vel, old, kind, sigma, epsilon, mine, local_sem, send_sem, row_sem, col_sem,
):
    me = Place()
    barrier = greet(me)
    local = [
        pltpu.make_async_copy(src, dst, local_sem.at[n])
        for n, (src, dst) in enumerate(
            (
                (pos_hbm, pos), (vel_hbm, vel), (old_hbm, old), (kind_hbm, kind),
                (sigma_hbm, sigma), (epsilon_hbm, epsilon), (pairs_hbm, pairs),
            )
        )
    ]
    for copy in local:
        copy.start()
    for copy in local[:4]:
        copy.wait()
    moved[...] = pos[...] + time_step * vel[...] + 0.5 * time_step * time_step * old[...]
    kinds = kind[...].astype(jnp.float32)
    for e in range(BPD):
        mine[4 * e : 4 * e + 3, :] = moved[:, BLK * e : BLK * (e + 1)]
        mine[4 * e + 3 : 4 * e + 4, :] = kinds[e : e + 1, :]
    packet = mine[...]
    row_group[pl.ds(pl.multiple_of(me.c * 16, 16), 16), :] = packet
    col_group[pl.ds(pl.multiple_of(me.r * 16, 16), 16), :] = packet
    pl.semaphore_wait(barrier, len(me.partners()))

    started = []

    def ship(src, group, sems, slot, device):
        copy = pltpu.make_async_remote_copy(
            src_ref=src,
            dst_ref=group.at[pl.ds(pl.multiple_of(slot * 16, 16), 16), :],
            send_sem=send_sem.at[len(started)],
            recv_sem=sems.at[slot],
            device_id=device,
            device_id_type=MESH,
        )
        copy.start()
        started.append(copy)

    def arrived(group, sems, slot):
        view = group.at[pl.ds(pl.multiple_of(slot * 16, 16), 16), :]
        pltpu.make_async_remote_copy(
            src_ref=view,
            dst_ref=view,
            send_sem=send_sem.at[0],
            recv_sem=sems.at[slot],
            device_id=me.at_core(),
            device_id_type=MESH,
        ).wait_recv()
        return view

    own_row = me.row_slot(me.zh, me.x, me.k)
    for zh in (me.z_to, me.z_from):
        ship(mine, col_group, col_sem, own_row, me.at_z(zh))
    for zl in me.zl_mates:
        ship(mine, row_group, row_sem, me.c, me.at_zl(zl))
    for x in me.x_mates:
        ship(mine, col_group, col_sem, own_row, me.at_x(x))
    for y in me.y_mates:
        ship(mine, row_group, row_sem, me.c, me.at_y(y))
    ship(mine, col_group, col_sem, own_row, me.at_core())

    for copy in local[4:]:
        copy.wait()
    lane = lax.broadcasted_iota(jnp.int32, (8, BLK), 1)
    sizes = jnp.zeros((8, BLK), jnp.float32)
    wells = jnp.zeros((8, BLK), jnp.float32)
    for n in range(sigma.shape[0]):
        sizes = jnp.where(lane == n, 0.5 * sigma[n], sizes)
        wells = jnp.where(lane == n, epsilon[n], wells)
    tables[0] = sizes
    tables[1] = math.sqrt(16.0 / cutoff_sq) * jnp.sqrt(wells)

    def spread(zh, relay=False, last=False):
        slot = me.row_slot(zh, me.x, me.k)
        view = arrived(col_group, col_sem, slot)
        if relay:
            ship(view, col_group, col_sem, slot, me.at_z(me.z_to))
        for x in me.x_mates:
            ship(view, col_group, col_sem, slot, me.at_x(x))
            if last:
                ship(view, col_group, col_sem, slot, me.at_x_other(x))
        ship(view, col_group, col_sem, slot, me.at_core())

    def share(zh, x):
        slot = me.row_slot(zh, x, me.k)
        view = arrived(col_group, col_sem, slot)
        ship(view, col_group, col_sem, slot, me.at_core())

    def fan_out(zl):
        slot = me.col_slot(zl, me.y)
        view = arrived(row_group, row_sem, slot)
        for y in me.y_mates:
            ship(view, row_group, row_sem, slot, me.at_y(y))

    def bound(group, middle, ends, slots):
        found = []
        for slot in slots:
            for h in range(2):
                both = group[pl.ds(pl.multiple_of(slot * 16 + 8 * h, 8), 8), :]
                low = jnp.broadcast_to(jnp.min(both, axis=1, keepdims=True), (8, BLK))
                high = jnp.broadcast_to(jnp.max(both, axis=1, keepdims=True), (8, BLK))
                middle[2 * slot + h] = 0.5 * (low + high)
                found.append((lane == 2 * slot + h, low, high))
        lows, highs = ends[0], ends[1]
        for here, low, high in found:
            lows = jnp.where(here, low, lows)
            highs = jnp.where(here, high, highs)
        ends[0], ends[1] = lows, highs

    def bound_rows(slots):
        bound(row_group, row_mid, row_ends, slots)

    def bound_cols(slots):
        bound(col_group, col_mid, col_ends, slots)

    def take_rows(slots):
        for slot in slots:
            arrived(row_group, row_sem, slot)
        bound_rows(slots)

    def take_cols(slots):
        for slot in slots:
            arrived(col_group, col_sem, slot)
        bound_cols(slots)

    for ends in (row_ends, col_ends):
        ends[...] = jnp.zeros_like(ends)
    bound_rows([me.c])
    bound_cols([own_row])
    for zl in me.zl_mates[1:]:
        fan_out(zl)
    for x in me.x_mates:
        share(me.zh, x)
    fan_out(me.zl_mates[0])
    bound_rows([me.col_slot(zl, me.y) for zl in me.zl_mates])
    bound_cols([me.row_slot(me.zh, x, me.k) for x in me.x_mates])
    spread(me.z_from, relay=True)
    spread(me.z_to)
    ends_z = (me.z_from, me.z_to)
    bound_cols([me.row_slot(zh, me.x, me.k) for zh in ends_z])
    xs = [me.x] + me.x_mates
    take_cols([me.row_slot(me.zh, x, 1 - me.k) for x in xs])
    take_rows([me.col_slot(me.zl, y) for y in me.y_mates])
    for x in me.x_mates:
        share(me.z_from, x)
        share(me.z_to, x)
    bound_cols([me.row_slot(zh, x, me.k) for x in me.x_mates for zh in ends_z])
    take_rows([me.col_slot(zl, y) for zl in me.zl_mates for y in me.y_mates])
    spread(me.z_far, last=True)
    take_cols([me.row_slot(zh, x, 1 - me.k) for x in xs for zh in ends_z])
    bound_cols([me.row_slot(me.z_far, me.x, me.k)])
    take_cols([me.row_slot(me.z_far, me.x, 1 - me.k)])
    take_cols([me.row_slot(me.z_far, x, k) for x in me.x_mates for k in (me.k, 1 - me.k)])
    for copy in started:
        copy.wait_send()


def split3(v):
    head = v.astype(jnp.bfloat16).astype(jnp.float32)
    rest = v - head
    mid = rest.astype(jnp.bfloat16).astype(jnp.float32)
    return head, mid, rest - mid


def pair_kernel(
    box_y, box_z, live, pairs, tables, row_group, col_group, row_mid, col_mid, row_ends, col_ends, moved_in,
    on_row, on_col, moved, rows, cols, row_acc, col_acc, listed, todo, k_parts, lefts, rights, sources, shifts, sem,
):
    f32, bf16 = jnp.float32, jnp.bfloat16
    moved[...] = moved_in[...]
    sub = lax.broadcasted_iota(jnp.int32, (8, BLK), 0)
    lane = lax.broadcasted_iota(jnp.int32, (8, BLK), 1)
    sizes, wells = tables[0], tables[1]
    kind_row = (sub == 3) | (sub == 7)
    box = jnp.where(sub == 0, BPD * cell_side, jnp.where(sub == 1, box_y, jnp.where(sub == 2, box_z, 1.0)))
    inverse_box = 1.0 / box

    def wrap(v):
        return v - box * jnp.floor(v * inverse_box + 0.5)

    def look_up(group, middle, index):
        g = index // 2
        mid = middle[g]
        both = group[pl.ds(pl.multiple_of(8 * g, 8), 8), :]
        odd = jnp.full((8, BLK), index % 2) == 1
        near = jnp.where(kind_row, both, both - mid)
        near = jnp.where(odd, pltpu.roll(near, 4, 0), near)
        mid = jnp.where(sub < 3, jnp.where(odd, pltpu.roll(mid, 4, 0), mid), 0.0)
        kinds = jnp.broadcast_to(near[3:4], (8, BLK)).astype(jnp.int32)
        size = jnp.take_along_axis(sizes, kinds, axis=1, mode="promise_in_bounds")
        well = jnp.take_along_axis(wells, kinds, axis=1, mode="promise_in_bounds")
        tile = jnp.where(sub < 3, near, jnp.where(sub == 3, size, jnp.where(sub == 4, well, 0.0)))
        return tile, mid

    firsts = jnp.broadcast_to(pairs[0:1, :], (8, BLK))
    seconds = jnp.broadcast_to(pairs[1:2, :], (8, BLK))

    def pick(bound, index):
        got = jnp.take_along_axis(bound, index >> 1, axis=1, mode="promise_in_bounds")
        return jnp.where((index & 1) == 1, pltpu.roll(got, 4, 0), got)

    xl, xh = pick(row_ends[0], firsts), pick(row_ends[1], firsts)
    yl, yh = pick(col_ends[0], seconds), pick(col_ends[1], seconds)
    apart = wrap(jnp.where(sub < 3, 0.5 * ((yl + yh) - (xl + xh)), 0.0))
    gap = jnp.abs(apart) - 0.5 * ((yh - yl) + (xh - xl))
    gap = jnp.where(sub < 3, jnp.maximum(gap, 0.0), 0.0)
    gap2 = jnp.sum(gap * gap, axis=0, keepdims=True)
    near_by = jnp.broadcast_to(gap2, (8, BLK)) < cutoff_sq + 0.01
    active = jnp.where(near_by & (lane < live[...]), 1.0, 0.0)
    big_sub = lax.broadcasted_iota(jnp.int32, (BLK, BLK), 0)
    big_lane = lax.broadcasted_iota(jnp.int32, (BLK, BLK), 1)
    across = (((1,), (1,)), ((), ()))
    down = (((1,), (0,)), ((), ()))

    def dot(u, v, dims):
        return lax.dot_general(u, v, dims, preferred_element_type=f32)

    upto = dot(jnp.where(big_lane <= big_sub, 1.0, 0.0).astype(bf16), active.astype(bf16), across)[:, 0:1]
    before = dot(jnp.where(big_lane < big_sub, 1.0, 0.0).astype(bf16), active.astype(bf16), across)[:, 0:1]
    place = big_lane.astype(f32)
    move = jnp.where((place >= before) & (place < upto), 1.0, 0.0).astype(bf16)
    both = jnp.where(sub == 0, firsts, seconds).astype(f32).astype(bf16)
    packed = dot(both, move, down)
    count = jnp.broadcast_to(jnp.sum(active, axis=1, keepdims=True), (8, BLK))
    spare = jnp.where(sub == 0, float(NA), float(NB))
    packed = jnp.where(lane.astype(f32) < count, packed, spare)
    listed[...] = jnp.where(sub == 2, count, packed).astype(jnp.int32)
    copy = pltpu.make_async_copy(listed, todo, sem)
    copy.start()
    row_acc[...] = jnp.zeros_like(row_acc)
    col_acc[...] = jnp.zeros_like(col_acc)
    copy.wait()
    total = todo[2, 0]
    row_id, col_id = lax.axis_index("row"), lax.axis_index("col")
    scale = 1.5 * cutoff_sq

    def force_sources(tile):
        well = tile[4:5]
        v = jnp.where(sub < 3, tile * well, jnp.where(sub == 3, well, 0.0))
        head, mid, low = split3(v)
        first = jnp.where(sub < 4, head, pltpu.roll(low, 4, 0))
        return jnp.concatenate([first, mid], axis=0).astype(bf16)

    def fold(v):
        v = v[0:8] + v[8:16]
        return v + pltpu.roll(v, 4, 0)

    def entry(p):
        valid = (p >= 0) & (p < total)
        q = jnp.clip(p, 0, BLK - 1)
        return jnp.where(valid, todo[0, q], NA), jnp.where(valid, todo[1, q], NB)

    def finish(n, p, vr, vc):
        a, b = entry(p)
        mine, theirs = rows[a], cols[b]
        shift = shifts[p + 4]
        vr, vc = fold(vr), fold(vc)
        fr = (vr + (shift - mine) * vr[3:4]) * mine[4:5]
        fc = (vc - (shift + theirs) * vc[3:4]) * theirs[4:5]
        same = (b // BPD == row_id) & (a == col_id * BPD + b % BPD)
        fc = fc * jnp.where(same, 0.0, 1.0)
        row_acc[a] = row_acc[a] + fr
        col_acc[b] = col_acc[b] + fc

    def pull(n, head, tail):
        px, py = sources[n, 0], sources[n, 1]
        px, py = jnp.concatenate([px, px], axis=1), jnp.concatenate([py, py], axis=1)
        return (
            dot(py, jnp.concatenate([head, tail], axis=1), across),
            dot(px, jnp.concatenate([head, tail], axis=0), down),
        )

    def coefficients(n, p, terms):
        for m in range(0, BLK, 16):
            w, soft, sig2 = [terms[m : m + 16, BLK * v : BLK * (v + 1)] for v in range(3)]
            w = jnp.maximum(w, 0.0)
            guess = pl.reciprocal(soft, approx=True)
            inv = guess * (2.0 - soft * guess)
            ratio = sig2 * inv
            u3 = ratio * ratio * ratio
            t = inv * w
            t1 = t + 1.0
            k = (t1 - u3 * (t1 + t)) * (u3 * w)
            high = k.astype(bf16)
            k_parts[n, 0, m : m + 16, :] = high
            k_parts[n, 1, m : m + 16, :] = (k - high.astype(f32)).astype(bf16)
        a, b = entry(p)
        sources[n, 0] = force_sources(rows[a])
        sources[n, 1] = force_sources(cols[b])

    def describe(n, p):
        a, b = entry(p)
        mine, near_mid = look_up(row_group, row_mid, jnp.minimum(a, NA - 1))
        theirs, far_mid = look_up(col_group, col_mid, jnp.minimum(b, NB - 1))
        rows[a] = mine
        cols[b] = theirs
        shift = wrap(far_mid - near_mid)
        shifts[p + 4] = shift
        other = theirs + shift
        sq = mine * mine
        norm = (sq[0:1] + sq[1:2] + sq[2:3]) * (1.0 / cutoff_sq)
        left = jnp.where(sub < 5, mine, jnp.where(sub == 5, norm, jnp.where(sub == 6, sq[3:4], 1.0)))
        head, mid, low = split3(left)
        lefts[n] = jnp.concatenate([head, head, head, mid, mid, low], axis=0).T.astype(bf16)
        sq = other * other
        norm = sq[0:1] + sq[1:2] + sq[2:3]
        size2 = sq[3:4]
        inv_c = 1.0 / scale
        for_w = jnp.where(
            sub < 3, other * (2.0 / cutoff_sq),
            jnp.where(sub == 5, -1.0, jnp.where(sub == 7, 1.0 - norm * (1.0 / cutoff_sq), 0.0)),
        )
        for_sig = jnp.where(
            sub == 3, other * (2.0 * inv_c), jnp.where(sub == 6, inv_c, jnp.where(sub == 7, size2 * inv_c, 0.0))
        )
        for_soft = jnp.where(
            sub < 3, other * (-2.0 * inv_c),
            jnp.where(sub == 5, cutoff_sq * inv_c, jnp.where(sub == 7, (norm + size2) * inv_c, for_sig)),
        )
        for m, right in enumerate((for_w, for_soft, for_sig)):
            head, mid, low = split3(right)
            rights[n, :, BLK * m : BLK * (m + 1)] = jnp.concatenate([head, mid, low, head, mid, head], axis=0).astype(bf16)

    def turn(g, carry):
        held = [(k_parts[n, 0], k_parts[n, 1]) for n in range(4)]
        terms = [dot(lefts[n], rights[n], down) for n in range(4)]
        for n in range(4):
            finish(n, 4 * (g - 1) + n, *pull(n, *held[n]))
        for n in range(4):
            coefficients(n, 4 * g + n, terms[n])
        for n in range(4):
            describe(n, 4 * (g + 1) + n)
        return carry

    groups = (total + 3) // 4
    for n in range(4):
        describe(n, n)
    lax.fori_loop(0, groups, turn, 0)
    for n in range(4):
        finish(n, 4 * (groups - 1) + n, *pull(n, k_parts[n, 0], k_parts[n, 1]))
    on_row[...] = row_acc[0:NA, 0:4, :]
    on_col[...] = col_acc[0:NB, 0:4, :]


def scatter_kernel(
    on_row, on_col, row_share, col_share,
    far_in, far_out, core_in, near_out, near_in, near_sum, z_relay, z_in, y_in, zl_out, zl_in,
    send_sem, far_sem, core_sem, near_sem, z_sem, y_sem, zl_sem,
):
    me = Place()
    barrier = greet(me)
    pl.semaphore_wait(barrier, len(me.partners()))
    started = []

    def ship(src, dst, sem, device):
        copy = pltpu.make_async_remote_copy(
            src_ref=src, dst_ref=dst, send_sem=send_sem.at[len(started)], recv_sem=sem,
            device_id=device, device_id_type=MESH,
        )
        copy.start()
        started.append(copy)

    def arrived(dst, sem):
        pltpu.make_async_remote_copy(
            src_ref=dst, dst_ref=dst, send_sem=send_sem.at[0], recv_sem=sem,
            device_id=me.at_core(), device_id_type=MESH,
        ).wait_recv()

    def far(x, k, device):
        ship(on_col.at[me.z_far, x, k], far_in.at[me.x * NK + me.k], far_sem.at[me.x * NK + me.k], device)

    for x in me.x_mates:
        far(x, me.k, me.at_x(x))
        far(x, 1 - me.k, me.at_x_other(x))
    far(me.x, 1 - me.k, me.at_core())
    near = [(me.zh + 3) % NZH, me.zh, (me.zh + 1) % NZH]
    j_from, j_to = 2 * me.k, 2 - 2 * me.k
    for j, zh in enumerate(near):
        ship(on_col.at[zh, :, 1 - me.k], core_in.at[j], core_sem.at[j], me.at_core())
    for y in me.y_mates:
        ship(on_row.at[:, y], y_in.at[me.y], y_sem.at[me.y], me.at_y(y))
    for j, zh in enumerate(near):
        arrived(core_in.at[j], core_sem.at[j])
        for x in me.x_mates:
            near_out[x, j] = on_col[zh, x, me.k] + core_in[j, x]
        near_sum[j] = on_col[zh, me.x, me.k] + core_in[j, me.x]
    for x in me.x_mates:
        ship(near_out.at[x], near_in.at[me.x], near_sem.at[me.x], me.at_x(x))
    total = on_col[me.z_far, me.x, me.k]
    order = [(me.x, 1 - me.k)]
    for x in (me.x_mates[1], me.x_mates[2], me.x_mates[0]):
        order += [(x, me.k), (x, 1 - me.k)]
    for x, k in order:
        arrived(far_in.at[x * NK + k], far_sem.at[x * NK + k])
        total = total + far_in[x * NK + k]
    far_out[...] = total
    ship(far_out, z_in.at[0], z_sem.at[0], me.at_z(me.z_to))

    for x in (me.x_mates[1], me.x_mates[2], me.x_mates[0]):
        arrived(near_in.at[x], near_sem.at[x])
    near_sum[...] = (
        near_sum[...] + near_in[me.x_mates[0]] + near_in[me.x_mates[1]] + near_in[me.x_mates[2]]
    )
    ship(near_sum.at[j_from], z_in.at[1], z_sem.at[1], me.at_z(me.z_from))

    total = on_row[:, me.y]
    for y in me.y_mates:
        arrived(y_in.at[y], y_sem.at[y])
        total = total + y_in[y]
    zl_out[...] = total
    for zl in me.zl_mates:
        ship(zl_out.at[zl], zl_in.at[me.zl], zl_sem.at[me.zl], me.at_zl(zl))

    arrived(z_in.at[0], z_sem.at[0])
    z_relay[...] = z_in[0] + near_sum[j_to]
    ship(z_relay, z_in.at[2], z_sem.at[2], me.at_z(me.z_to))
    row_total, col_total = zl_out[me.zl], near_sum[1]
    for zl in me.zl_mates:
        arrived(zl_in.at[zl], zl_sem.at[zl])
        row_total = row_total + zl_in[zl]
    for e in range(BPD):
        row_share[:, BLK * e : BLK * (e + 1)] = row_total[e, 0:3]
    arrived(z_in.at[1], z_sem.at[1])
    col_total = col_total + z_in[1]
    arrived(z_in.at[2], z_sem.at[2])
    col_total = col_total + z_in[2]
    for e in range(BPD):
        col_share[:, BLK * e : BLK * (e + 1)] = col_total[e, 0:3]
    for copy in started:
        copy.wait_send()


def body(positions, velocities, old_forces, types, sigma_table, epsilon_table, pairs, live):
    f32 = jnp.float32
    dma = pltpu.SemaphoreType.DMA
    vmem = pl.BlockSpec(memory_space=VMEM)
    hbm = pl.BlockSpec(memory_space=pltpu.HBM)
    i32 = jnp.int32
    coords = positions.shape
    row_group, col_group, moved_near, pairs_near, tables, *boxes = pl.pallas_call(
        gather_kernel,
        out_shape=(
            jax.ShapeDtypeStruct((NA * 4, BLK), f32),
            jax.ShapeDtypeStruct((NB * 4, BLK), f32),
            jax.ShapeDtypeStruct(coords, f32),
            jax.ShapeDtypeStruct((2, BLK), i32),
            jax.ShapeDtypeStruct((2, 8, BLK), f32),
            jax.ShapeDtypeStruct((NA // 2, 8, BLK), f32),
            jax.ShapeDtypeStruct((NB // 2, 8, BLK), f32),
            jax.ShapeDtypeStruct((2, 8, BLK), f32),
            jax.ShapeDtypeStruct((2, 8, BLK), f32),
        ),
        in_specs=[hbm] * 7,
        out_specs=(vmem,) * 9,
        scratch_shapes=[
            VMEM(coords, f32),
            VMEM(coords, f32),
            VMEM(coords, f32),
            VMEM((BPD, BLK), i32),
            pltpu.SMEM(sigma_table.shape, f32),
            pltpu.SMEM(epsilon_table.shape, f32),
            VMEM((4 * BPD, BLK), f32),
            dma((7,)),
            dma((48,)),
            dma((COLS,)),
            dma((ROWS,)),
        ],
        compiler_params=pltpu.CompilerParams(collective_id=0, has_side_effects=True, vmem_limit_bytes=8 << 20),
        name="gather",
    )(
        *[
            pltpu.with_memory_space_constraint(v, pltpu.HBM)
            for v in (
                positions, velocities, old_forces, types.reshape(BPD, BLK), sigma_table, epsilon_table,
                pairs.reshape(2, BLK),
            )
        ]
    )

    def pair_call(*refs):
        return pair_kernel(ROWS * cell_side, COLS * cell_side, *refs)

    on_row, on_col, moved = pl.pallas_call(
        pair_call,
        out_shape=(
            jax.ShapeDtypeStruct((NA, 4, BLK), f32),
            jax.ShapeDtypeStruct((NB, 4, BLK), f32),
            jax.ShapeDtypeStruct(positions.shape, f32),
        ),
        in_specs=[vmem] * 10,
        out_specs=(vmem, vmem, vmem),
        scratch_shapes=[
            VMEM((NA + 1, 8, BLK), f32),
            VMEM((NB + 1, 8, BLK), f32),
            VMEM((NA + 1, 8, BLK), f32),
            VMEM((NB + 1, 8, BLK), f32),
            VMEM((8, BLK), jnp.int32),
            pltpu.SMEM((8, BLK), jnp.int32),
            VMEM((4, 2, BLK, BLK), jnp.bfloat16),
            VMEM((4, BLK, 48), jnp.bfloat16),
            VMEM((4, 48, 3 * BLK), jnp.bfloat16),
            VMEM((4, 2, 16, BLK), jnp.bfloat16),
            VMEM((BLK + 12, 8, BLK), f32),
            dma,
        ],
        compiler_params=pltpu.CompilerParams(vmem_limit_bytes=16 << 20),
        name="pairs",
    )(
        jnp.broadcast_to(live, (8, BLK)), pairs_near, tables, row_group, col_group, *boxes, moved_near,
    )

    tile = (BPD, 4, BLK)
    row_share, col_share = pl.pallas_call(
        scatter_kernel,
        out_shape=(jax.ShapeDtypeStruct(positions.shape, f32), jax.ShapeDtypeStruct(positions.shape, f32)),
        in_specs=[vmem] * 2,
        out_specs=(vmem, vmem),
        scratch_shapes=[
            VMEM((NX * NK,) + tile, f32),
            VMEM(tile, f32),
            VMEM((3, NX) + tile, f32),
            VMEM((NX, 3) + tile, f32),
            VMEM((NX, 3) + tile, f32),
            VMEM((3,) + tile, f32),
            VMEM(tile, f32),
            VMEM((3,) + tile, f32),
            VMEM((NY, NZL) + tile, f32),
            VMEM((NZL,) + tile, f32),
            VMEM((NZL,) + tile, f32),
            dma((24,)),
            dma((NX * NK,)),
            dma((3,)),
            dma((NX,)),
            dma((3,)),
            dma((NY,)),
            dma((NZL,)),
        ],
        compiler_params=pltpu.CompilerParams(collective_id=1, has_side_effects=True, vmem_limit_bytes=8 << 20),
        name="scatter",
    )(
        on_row.reshape((NZL, NY) + tile),
        on_col.reshape((NZH, NX, NK) + tile),
    )
    new_forces = row_share + col_share
    new_velocities = velocities + 0.5 * time_step * (old_forces + new_forces)
    return moved, new_velocities, new_forces


def solution(mesh):
    in_specs = (
        P(None, ("row", "col")),
        P(None, ("row", "col")),
        P(None, ("row", "col")),
        P(("row", "col")),
        P(),
        P(),
        P("row", "col", None, None),
        P("row", "col"),
    )
    out_specs = (P(None, ("row", "col")), P(None, ("row", "col")), P(None, ("row", "col")))
    return jax.shard_map(body, mesh=mesh, in_specs=in_specs, out_specs=out_specs, check_vma=False)
```

```python
import math

import jax
import jax.numpy as jnp
from jax import lax
from jax.experimental import pallas as pl
from jax.experimental.pallas import tpu as pltpu
from jax.sharding import PartitionSpec as P

BLK = 128
BPD = 4
NZH, NX, NK = 4, 4, 2
NZL, NY = 4, 4
ROWS, COLS = NZH * NX * NK, NZL * NY
NA, NB = COLS * BPD, ROWS * BPD

time_step = 0.05
cell_side = 5.3
cutoff_sq = 6.25

MESH = pl.DeviceIdType.MESH
VMEM = pltpu.VMEM


class Place:
    def __init__(self):
        r, c = lax.axis_index("row"), lax.axis_index("col")
        self.r, self.c = r, c
        self.zh, self.x, self.k = r // (NX * NK), (r // NK) % NX, r % NK
        self.zl, self.y = c // NY, c % NY
        self.z_from = (self.zh + 3 - 2 * self.k) % NZH
        self.z_to = (self.zh + 1 + 2 * self.k) % NZH
        self.z_far = (self.zh + 2) % NZH
        self.x_mates = [(self.x + s) % NX for s in (2, 1, 3)]
        self.zl_mates = [(self.zl + s) % NZL for s in (2, 1, 3)]
        self.y_mates = [(self.y + s) % NY for s in (2, 1, 3)]

    def row_slot(self, zh, x, k):
        return (zh * NX + x) * NK + k

    def col_slot(self, zl, y):
        return zl * NY + y

    def at_z(self, zh):
        return (self.row_slot(zh, self.x, self.k), self.c)

    def at_x(self, x):
        return (self.row_slot(self.zh, x, self.k), self.c)

    def at_x_other(self, x):
        return (self.row_slot(self.zh, x, 1 - self.k), self.c)

    def at_core(self):
        return (self.row_slot(self.zh, self.x, 1 - self.k), self.c)

    def at_zl(self, zl):
        return (self.r, self.col_slot(zl, self.y))

    def at_y(self, y):
        return (self.r, self.col_slot(self.zl, y))

    def partners(self):
        return (
            [self.at_z(self.z_from), self.at_z(self.z_to), self.at_core()]
            + [self.at_x(x) for x in self.x_mates]
            + [self.at_x_other(x) for x in self.x_mates]
            + [self.at_zl(z) for z in self.zl_mates]
            + [self.at_y(y) for y in self.y_mates]
        )


def greet(me):
    barrier = pltpu.get_barrier_semaphore()
    for device in me.partners():
        pl.semaphore_signal(barrier, inc=1, device_id=device, device_id_type=MESH)
    return barrier


def gather_kernel(
    pos_hbm, vel_hbm, old_hbm, kind_hbm, sigma_hbm, epsilon_hbm, pairs_hbm,
    row_group, col_group, moved, pairs, tables, row_mid, col_mid, row_ends, col_ends,
    pos, vel, old, kind, sigma, epsilon, mine, local_sem, send_sem, row_sem, col_sem,
):
    me = Place()
    barrier = greet(me)
    local = [
        pltpu.make_async_copy(src, dst, local_sem.at[n])
        for n, (src, dst) in enumerate(
            (
                (pos_hbm, pos), (vel_hbm, vel), (old_hbm, old), (kind_hbm, kind),
                (sigma_hbm, sigma), (epsilon_hbm, epsilon), (pairs_hbm, pairs),
            )
        )
    ]
    for copy in local:
        copy.start()
    for copy in local[:4]:
        copy.wait()
    moved[...] = pos[...] + time_step * vel[...] + 0.5 * time_step * time_step * old[...]
    kinds = kind[...].astype(jnp.float32)
    for e in range(BPD):
        mine[4 * e : 4 * e + 3, :] = moved[:, BLK * e : BLK * (e + 1)]
        mine[4 * e + 3 : 4 * e + 4, :] = kinds[e : e + 1, :]
    packet = mine[...]
    row_group[pl.ds(pl.multiple_of(me.c * 16, 16), 16), :] = packet
    col_group[pl.ds(pl.multiple_of(me.r * 16, 16), 16), :] = packet
    pl.semaphore_wait(barrier, len(me.partners()))

    started = []

    def ship(src, group, sems, slot, device):
        copy = pltpu.make_async_remote_copy(
            src_ref=src,
            dst_ref=group.at[pl.ds(pl.multiple_of(slot * 16, 16), 16), :],
            send_sem=send_sem.at[len(started)],
            recv_sem=sems.at[slot],
            device_id=device,
            device_id_type=MESH,
        )
        copy.start()
        started.append(copy)

    def arrived(group, sems, slot):
        view = group.at[pl.ds(pl.multiple_of(slot * 16, 16), 16), :]
        pltpu.make_async_remote_copy(
            src_ref=view,
            dst_ref=view,
            send_sem=send_sem.at[0],
            recv_sem=sems.at[slot],
            device_id=me.at_core(),
            device_id_type=MESH,
        ).wait_recv()
        return view

    own_row = me.row_slot(me.zh, me.x, me.k)
    for zh in (me.z_to, me.z_from):
        ship(mine, col_group, col_sem, own_row, me.at_z(zh))
    for zl in me.zl_mates:
        ship(mine, row_group, row_sem, me.c, me.at_zl(zl))
    for x in me.x_mates:
        ship(mine, col_group, col_sem, own_row, me.at_x(x))
    for y in me.y_mates:
        ship(mine, row_group, row_sem, me.c, me.at_y(y))
    ship(mine, col_group, col_sem, own_row, me.at_core())

    for copy in local[4:]:
        copy.wait()
    lane = lax.broadcasted_iota(jnp.int32, (8, BLK), 1)
    sizes = jnp.zeros((8, BLK), jnp.float32)
    wells = jnp.zeros((8, BLK), jnp.float32)
    for n in range(sigma.shape[0]):
        sizes = jnp.where(lane == n, 0.5 * sigma[n], sizes)
        wells = jnp.where(lane == n, epsilon[n], wells)
    tables[0] = sizes
    tables[1] = math.sqrt(16.0 / cutoff_sq) * jnp.sqrt(wells)

    def spread(zh, relay=False, last=False):
        slot = me.row_slot(zh, me.x, me.k)
        view = arrived(col_group, col_sem, slot)
        if relay:
            ship(view, col_group, col_sem, slot, me.at_z(me.z_to))
        for x in me.x_mates:
            ship(view, col_group, col_sem, slot, me.at_x(x))
            if last:
                ship(view, col_group, col_sem, slot, me.at_x_other(x))
        ship(view, col_group, col_sem, slot, me.at_core())

    def share(zh, x):
        slot = me.row_slot(zh, x, me.k)
        view = arrived(col_group, col_sem, slot)
        ship(view, col_group, col_sem, slot, me.at_core())

    def fan_out(zl):
        slot = me.col_slot(zl, me.y)
        view = arrived(row_group, row_sem, slot)
        for y in me.y_mates:
            ship(view, row_group, row_sem, slot, me.at_y(y))

    def bound(group, middle, ends, slots):
        found = []
        for slot in slots:
            for h in range(2):
                both = group[pl.ds(pl.multiple_of(slot * 16 + 8 * h, 8), 8), :]
                low = jnp.broadcast_to(jnp.min(both, axis=1, keepdims=True), (8, BLK))
                high = jnp.broadcast_to(jnp.max(both, axis=1, keepdims=True), (8, BLK))
                middle[2 * slot + h] = 0.5 * (low + high)
                found.append((lane == 2 * slot + h, low, high))
        lows, highs = ends[0], ends[1]
        for here, low, high in found:
            lows = jnp.where(here, low, lows)
            highs = jnp.where(here, high, highs)
        ends[0], ends[1] = lows, highs

    def bound_rows(slots):
        bound(row_group, row_mid, row_ends, slots)

    def bound_cols(slots):
        bound(col_group, col_mid, col_ends, slots)

    def take_rows(slots):
        for slot in slots:
            arrived(row_group, row_sem, slot)
        bound_rows(slots)

    def take_cols(slots):
        for slot in slots:
            arrived(col_group, col_sem, slot)
        bound_cols(slots)

    for ends in (row_ends, col_ends):
        ends[...] = jnp.zeros_like(ends)
    bound_rows([me.c])
    bound_cols([own_row])
    for zl in me.zl_mates[1:]:
        fan_out(zl)
    for x in me.x_mates:
        share(me.zh, x)
    fan_out(me.zl_mates[0])
    bound_rows([me.col_slot(zl, me.y) for zl in me.zl_mates])
    bound_cols([me.row_slot(me.zh, x, me.k) for x in me.x_mates])
    spread(me.z_from, relay=True)
    spread(me.z_to)
    ends_z = (me.z_from, me.z_to)
    bound_cols([me.row_slot(zh, me.x, me.k) for zh in ends_z])
    xs = [me.x] + me.x_mates
    take_cols([me.row_slot(me.zh, x, 1 - me.k) for x in xs])
    take_rows([me.col_slot(me.zl, y) for y in me.y_mates])
    for x in me.x_mates:
        share(me.z_from, x)
        share(me.z_to, x)
    bound_cols([me.row_slot(zh, x, me.k) for x in me.x_mates for zh in ends_z])
    take_rows([me.col_slot(zl, y) for zl in me.zl_mates for y in me.y_mates])
    spread(me.z_far, last=True)
    take_cols([me.row_slot(zh, x, 1 - me.k) for x in xs for zh in ends_z])
    bound_cols([me.row_slot(me.z_far, me.x, me.k)])
    take_cols([me.row_slot(me.z_far, me.x, 1 - me.k)])
    take_cols([me.row_slot(me.z_far, x, k) for x in me.x_mates for k in (me.k, 1 - me.k)])
    for copy in started:
        copy.wait_send()


def split3(v):
    head = v.astype(jnp.bfloat16).astype(jnp.float32)
    rest = v - head
    mid = rest.astype(jnp.bfloat16).astype(jnp.float32)
    return head, mid, rest - mid


def pair_kernel(
    box_y, box_z, live, pairs, tables, row_group, col_group, row_mid, col_mid, row_ends, col_ends, moved_in,
    on_row, on_col, moved, rows, cols, row_acc, col_acc, listed, todo, k_parts, lefts, rights, sources, shifts, sem,
):
    f32, bf16 = jnp.float32, jnp.bfloat16
    moved[...] = moved_in[...]
    sub = lax.broadcasted_iota(jnp.int32, (8, BLK), 0)
    lane = lax.broadcasted_iota(jnp.int32, (8, BLK), 1)
    sizes, wells = tables[0], tables[1]
    kind_row = (sub == 3) | (sub == 7)
    box = jnp.where(sub == 0, BPD * cell_side, jnp.where(sub == 1, box_y, jnp.where(sub == 2, box_z, 1.0)))
    inverse_box = 1.0 / box

    def wrap(v):
        return v - box * jnp.floor(v * inverse_box + 0.5)

    def look_up(group, middle, index):
        g = index // 2
        mid = middle[g]
        both = group[pl.ds(pl.multiple_of(8 * g, 8), 8), :]
        odd = jnp.full((8, BLK), index % 2) == 1
        near = jnp.where(kind_row, both, both - mid)
        near = jnp.where(odd, pltpu.roll(near, 4, 0), near)
        mid = jnp.where(sub < 3, jnp.where(odd, pltpu.roll(mid, 4, 0), mid), 0.0)
        kinds = jnp.broadcast_to(near[3:4], (8, BLK)).astype(jnp.int32)
        size = jnp.take_along_axis(sizes, kinds, axis=1, mode="promise_in_bounds")
        well = jnp.take_along_axis(wells, kinds, axis=1, mode="promise_in_bounds")
        tile = jnp.where(sub < 3, near, jnp.where(sub == 3, size, jnp.where(sub == 4, well, 0.0)))
        return tile, mid

    firsts = jnp.broadcast_to(pairs[0:1, :], (8, BLK))
    seconds = jnp.broadcast_to(pairs[1:2, :], (8, BLK))

    def pick(bound, index):
        got = jnp.take_along_axis(bound, index >> 1, axis=1, mode="promise_in_bounds")
        return jnp.where((index & 1) == 1, pltpu.roll(got, 4, 0), got)

    xl, xh = pick(row_ends[0], firsts), pick(row_ends[1], firsts)
    yl, yh = pick(col_ends[0], seconds), pick(col_ends[1], seconds)
    apart = wrap(jnp.where(sub < 3, 0.5 * ((yl + yh) - (xl + xh)), 0.0))
    gap = jnp.abs(apart) - 0.5 * ((yh - yl) + (xh - xl))
    gap = jnp.where(sub < 3, jnp.maximum(gap, 0.0), 0.0)
    gap2 = jnp.sum(gap * gap, axis=0, keepdims=True)
    near_by = jnp.broadcast_to(gap2, (8, BLK)) < cutoff_sq + 0.01
    active = jnp.where(near_by & (lane < live[...]), 1.0, 0.0)
    big_sub = lax.broadcasted_iota(jnp.int32, (BLK, BLK), 0)
    big_lane = lax.broadcasted_iota(jnp.int32, (BLK, BLK), 1)
    across = (((1,), (1,)), ((), ()))
    down = (((1,), (0,)), ((), ()))

    def dot(u, v, dims):
        return lax.dot_general(u, v, dims, preferred_element_type=f32)

    upto = dot(jnp.where(big_lane <= big_sub, 1.0, 0.0).astype(bf16), active.astype(bf16), across)[:, 0:1]
    before = dot(jnp.where(big_lane < big_sub, 1.0, 0.0).astype(bf16), active.astype(bf16), across)[:, 0:1]
    place = big_lane.astype(f32)
    move = jnp.where((place >= before) & (place < upto), 1.0, 0.0).astype(bf16)
    both = jnp.where(sub == 0, firsts, seconds).astype(f32).astype(bf16)
    packed = dot(both, move, down)
    count = jnp.broadcast_to(jnp.sum(active, axis=1, keepdims=True), (8, BLK))
    spare = jnp.where(sub == 0, float(NA), float(NB))
    packed = jnp.where(lane.astype(f32) < count, packed, spare)
    listed[...] = jnp.where(sub == 2, count, packed).astype(jnp.int32)
    copy = pltpu.make_async_copy(listed, todo, sem)
    copy.start()
    row_acc[...] = jnp.zeros_like(row_acc)
    col_acc[...] = jnp.zeros_like(col_acc)
    copy.wait()
    total = todo[2, 0]
    row_id, col_id = lax.axis_index("row"), lax.axis_index("col")
    scale = 1.5 * cutoff_sq

    def force_sources(tile):
        well = tile[4:5]
        v = jnp.where(sub < 3, tile * well, jnp.where(sub == 3, well, 0.0))
        head, mid, low = split3(v)
        first = jnp.where(sub < 4, head, pltpu.roll(low, 4, 0))
        return jnp.concatenate([first, mid], axis=0).astype(bf16)

    def fold(v):
        v = v[0:8] + v[8:16]
        return v + pltpu.roll(v, 4, 0)

    def entry(p):
        valid = (p >= 0) & (p < total)
        q = jnp.clip(p, 0, BLK - 1)
        return jnp.where(valid, todo[0, q], NA), jnp.where(valid, todo[1, q], NB)

    def finish(n, p, vr, vc):
        a, b = entry(p)
        mine, theirs = rows[a], cols[b]
        shift = shifts[p + 4]
        vr, vc = fold(vr), fold(vc)
        fr = (vr + (shift - mine) * vr[3:4]) * mine[4:5]
        fc = (vc - (shift + theirs) * vc[3:4]) * theirs[4:5]
        same = (b // BPD == row_id) & (a == col_id * BPD + b % BPD)
        fc = fc * jnp.where(same, 0.0, 1.0)
        row_acc[a] = row_acc[a] + fr
        col_acc[b] = col_acc[b] + fc

    def pull(n, head, tail):
        px, py = sources[n, 0], sources[n, 1]
        px, py = jnp.concatenate([px, px], axis=1), jnp.concatenate([py, py], axis=1)
        return (
            dot(py, jnp.concatenate([head, tail], axis=1), across),
            dot(px, jnp.concatenate([head, tail], axis=0), down),
        )

    def coefficients(n, p, terms):
        for m in range(0, BLK, 16):
            w, soft, sig2 = [terms[m : m + 16, BLK * v : BLK * (v + 1)] for v in range(3)]
            w = jnp.maximum(w, 0.0)
            guess = pl.reciprocal(soft, approx=True)
            inv = guess * (2.0 - soft * guess)
            ratio = sig2 * inv
            u3 = ratio * ratio * ratio
            t = inv * w
            t1 = t + 1.0
            k = (t1 - u3 * (t1 + t)) * (u3 * w)
            high = k.astype(bf16)
            k_parts[n, 0, m : m + 16, :] = high
            k_parts[n, 1, m : m + 16, :] = (k - high.astype(f32)).astype(bf16)
        a, b = entry(p)
        sources[n, 0] = force_sources(rows[a])
        sources[n, 1] = force_sources(cols[b])

    def describe(n, p):
        a, b = entry(p)
        mine, near_mid = look_up(row_group, row_mid, jnp.minimum(a, NA - 1))
        theirs, far_mid = look_up(col_group, col_mid, jnp.minimum(b, NB - 1))
        rows[a] = mine
        cols[b] = theirs
        shift = wrap(far_mid - near_mid)
        shifts[p + 4] = shift
        other = theirs + shift
        sq = mine * mine
        norm = (sq[0:1] + sq[1:2] + sq[2:3]) * (1.0 / cutoff_sq)
        left = jnp.where(sub < 5, mine, jnp.where(sub == 5, norm, jnp.where(sub == 6, sq[3:4], 1.0)))
        head, mid, low = split3(left)
        lefts[n] = jnp.concatenate([head, head, head, mid, mid, low], axis=0).T.astype(bf16)
        sq = other * other
        norm = sq[0:1] + sq[1:2] + sq[2:3]
        size2 = sq[3:4]
        inv_c = 1.0 / scale
        for_w = jnp.where(
            sub < 3, other * (2.0 / cutoff_sq),
            jnp.where(sub == 5, -1.0, jnp.where(sub == 7, 1.0 - norm * (1.0 / cutoff_sq), 0.0)),
        )
        for_sig = jnp.where(
            sub == 3, other * (2.0 * inv_c), jnp.where(sub == 6, inv_c, jnp.where(sub == 7, size2 * inv_c, 0.0))
        )
        for_soft = jnp.where(
            sub < 3, other * (-2.0 * inv_c),
            jnp.where(sub == 5, cutoff_sq * inv_c, jnp.where(sub == 7, (norm + size2) * inv_c, for_sig)),
        )
        for m, right in enumerate((for_w, for_soft, for_sig)):
            head, mid, low = split3(right)
            rights[n, :, BLK * m : BLK * (m + 1)] = jnp.concatenate([head, mid, low, head, mid, head], axis=0).astype(bf16)

    def turn(g, carry):
        held = [(k_parts[n, 0], k_parts[n, 1]) for n in range(4)]
        terms = [dot(lefts[n], rights[n], down) for n in range(4)]
        for n in range(4):
            finish(n, 4 * (g - 1) + n, *pull(n, *held[n]))
        for n in range(4):
            coefficients(n, 4 * g + n, terms[n])
        for n in range(4):
            describe(n, 4 * (g + 1) + n)
        return carry

    groups = (total + 3) // 4
    for n in range(4):
        describe(n, n)
    lax.fori_loop(0, groups, turn, 0)
    for n in range(4):
        finish(n, 4 * (groups - 1) + n, *pull(n, k_parts[n, 0], k_parts[n, 1]))
    on_row[...] = row_acc[0:NA, 0:4, :]
    on_col[...] = col_acc[0:NB, 0:4, :]


def scatter_kernel(
    on_row, on_col, row_share, col_share,
    far_in, far_out, core_in, near_out, near_in, near_sum, z_relay, z_in, y_in, zl_out, zl_in,
    send_sem, far_sem, core_sem, near_sem, z_sem, y_sem, zl_sem,
):
    me = Place()
    barrier = greet(me)
    pl.semaphore_wait(barrier, len(me.partners()))
    started = []

    def ship(src, dst, sem, device):
        copy = pltpu.make_async_remote_copy(
            src_ref=src, dst_ref=dst, send_sem=send_sem.at[len(started)], recv_sem=sem,
            device_id=device, device_id_type=MESH,
        )
        copy.start()
        started.append(copy)

    def arrived(dst, sem):
        pltpu.make_async_remote_copy(
            src_ref=dst, dst_ref=dst, send_sem=send_sem.at[0], recv_sem=sem,
            device_id=me.at_core(), device_id_type=MESH,
        ).wait_recv()

    def far(x, k, device):
        ship(on_col.at[me.z_far, x, k], far_in.at[me.x * NK + me.k], far_sem.at[me.x * NK + me.k], device)

    for x in me.x_mates:
        far(x, me.k, me.at_x(x))
        far(x, 1 - me.k, me.at_x_other(x))
    far(me.x, 1 - me.k, me.at_core())
    near = [(me.zh + 3) % NZH, me.zh, (me.zh + 1) % NZH]
    j_from, j_to = 2 * me.k, 2 - 2 * me.k
    for j, zh in enumerate(near):
        ship(on_col.at[zh, :, 1 - me.k], core_in.at[j], core_sem.at[j], me.at_core())
    for j, zh in enumerate(near):
        arrived(core_in.at[j], core_sem.at[j])
        for x in me.x_mates:
            near_out[x, j] = on_col[zh, x, me.k] + core_in[j, x]
        near_sum[j] = on_col[zh, me.x, me.k] + core_in[j, me.x]
    for x in me.x_mates:
        ship(near_out.at[x], near_in.at[me.x], near_sem.at[me.x], me.at_x(x))
    for y in me.y_mates:
        ship(on_row.at[:, y], y_in.at[me.y], y_sem.at[me.y], me.at_y(y))
    total = on_col[me.z_far, me.x, me.k]
    order = [(me.x, 1 - me.k)]
    for x in (me.x_mates[1], me.x_mates[2], me.x_mates[0]):
        order += [(x, me.k), (x, 1 - me.k)]
    for x, k in order:
        arrived(far_in.at[x * NK + k], far_sem.at[x * NK + k])
        total = total + far_in[x * NK + k]
    far_out[...] = total
    ship(far_out, z_in.at[0], z_sem.at[0], me.at_z(me.z_to))

    for x in (me.x_mates[1], me.x_mates[2], me.x_mates[0]):
        arrived(near_in.at[x], near_sem.at[x])
    near_sum[...] = (
        near_sum[...] + near_in[me.x_mates[0]] + near_in[me.x_mates[1]] + near_in[me.x_mates[2]]
    )
    ship(near_sum.at[j_from], z_in.at[1], z_sem.at[1], me.at_z(me.z_from))

    total = on_row[:, me.y]
    for y in me.y_mates:
        arrived(y_in.at[y], y_sem.at[y])
        total = total + y_in[y]
    zl_out[...] = total
    for zl in me.zl_mates:
        ship(zl_out.at[zl], zl_in.at[me.zl], zl_sem.at[me.zl], me.at_zl(zl))

    arrived(z_in.at[0], z_sem.at[0])
    z_relay[...] = z_in[0] + near_sum[j_to]
    ship(z_relay, z_in.at[2], z_sem.at[2], me.at_z(me.z_to))
    row_total, col_total = zl_out[me.zl], near_sum[1]
    for zl in me.zl_mates:
        arrived(zl_in.at[zl], zl_sem.at[zl])
        row_total = row_total + zl_in[zl]
    for e in range(BPD):
        row_share[:, BLK * e : BLK * (e + 1)] = row_total[e, 0:3]
    arrived(z_in.at[1], z_sem.at[1])
    col_total = col_total + z_in[1]
    arrived(z_in.at[2], z_sem.at[2])
    col_total = col_total + z_in[2]
    for e in range(BPD):
        col_share[:, BLK * e : BLK * (e + 1)] = col_total[e, 0:3]
    for copy in started:
        copy.wait_send()


def body(positions, velocities, old_forces, types, sigma_table, epsilon_table, pairs, live):
    f32 = jnp.float32
    dma = pltpu.SemaphoreType.DMA
    vmem = pl.BlockSpec(memory_space=VMEM)
    hbm = pl.BlockSpec(memory_space=pltpu.HBM)
    i32 = jnp.int32
    coords = positions.shape
    row_group, col_group, moved_near, pairs_near, tables, *boxes = pl.pallas_call(
        gather_kernel,
        out_shape=(
            jax.ShapeDtypeStruct((NA * 4, BLK), f32),
            jax.ShapeDtypeStruct((NB * 4, BLK), f32),
            jax.ShapeDtypeStruct(coords, f32),
            jax.ShapeDtypeStruct((2, BLK), i32),
            jax.ShapeDtypeStruct((2, 8, BLK), f32),
            jax.ShapeDtypeStruct((NA // 2, 8, BLK), f32),
            jax.ShapeDtypeStruct((NB // 2, 8, BLK), f32),
            jax.ShapeDtypeStruct((2, 8, BLK), f32),
            jax.ShapeDtypeStruct((2, 8, BLK), f32),
        ),
        in_specs=[hbm] * 7,
        out_specs=(vmem,) * 9,
        scratch_shapes=[
            VMEM(coords, f32),
            VMEM(coords, f32),
            VMEM(coords, f32),
            VMEM((BPD, BLK), i32),
            pltpu.SMEM(sigma_table.shape, f32),
            pltpu.SMEM(epsilon_table.shape, f32),
            VMEM((4 * BPD, BLK), f32),
            dma((7,)),
            dma((48,)),
            dma((COLS,)),
            dma((ROWS,)),
        ],
        compiler_params=pltpu.CompilerParams(collective_id=0, has_side_effects=True, vmem_limit_bytes=8 << 20),
        name="gather",
    )(
        *[
            pltpu.with_memory_space_constraint(v, pltpu.HBM)
            for v in (
                positions, velocities, old_forces, types.reshape(BPD, BLK), sigma_table, epsilon_table,
                pairs.reshape(2, BLK),
            )
        ]
    )

    def pair_call(*refs):
        return pair_kernel(ROWS * cell_side, COLS * cell_side, *refs)

    on_row, on_col, moved = pl.pallas_call(
        pair_call,
        out_shape=(
            jax.ShapeDtypeStruct((NA, 4, BLK), f32),
            jax.ShapeDtypeStruct((NB, 4, BLK), f32),
            jax.ShapeDtypeStruct(positions.shape, f32),
        ),
        in_specs=[vmem] * 10,
        out_specs=(vmem, vmem, vmem),
        scratch_shapes=[
            VMEM((NA + 1, 8, BLK), f32),
            VMEM((NB + 1, 8, BLK), f32),
            VMEM((NA + 1, 8, BLK), f32),
            VMEM((NB + 1, 8, BLK), f32),
            VMEM((8, BLK), jnp.int32),
            pltpu.SMEM((8, BLK), jnp.int32),
            VMEM((4, 2, BLK, BLK), jnp.bfloat16),
            VMEM((4, BLK, 48), jnp.bfloat16),
            VMEM((4, 48, 3 * BLK), jnp.bfloat16),
            VMEM((4, 2, 16, BLK), jnp.bfloat16),
            VMEM((BLK + 12, 8, BLK), f32),
            dma,
        ],
        compiler_params=pltpu.CompilerParams(vmem_limit_bytes=16 << 20),
        name="pairs",
    )(
        jnp.broadcast_to(live, (8, BLK)), pairs_near, tables, row_group, col_group, *boxes, moved_near,
    )

    tile = (BPD, 4, BLK)
    row_share, col_share = pl.pallas_call(
        scatter_kernel,
        out_shape=(jax.ShapeDtypeStruct(positions.shape, f32), jax.ShapeDtypeStruct(positions.shape, f32)),
        in_specs=[vmem] * 2,
        out_specs=(vmem, vmem),
        scratch_shapes=[
            VMEM((NX * NK,) + tile, f32),
            VMEM(tile, f32),
            VMEM((3, NX) + tile, f32),
            VMEM((NX, 3) + tile, f32),
            VMEM((NX, 3) + tile, f32),
            VMEM((3,) + tile, f32),
            VMEM(tile, f32),
            VMEM((3,) + tile, f32),
            VMEM((NY, NZL) + tile, f32),
            VMEM((NZL,) + tile, f32),
            VMEM((NZL,) + tile, f32),
            dma((24,)),
            dma((NX * NK,)),
            dma((3,)),
            dma((NX,)),
            dma((3,)),
            dma((NY,)),
            dma((NZL,)),
        ],
        compiler_params=pltpu.CompilerParams(collective_id=1, has_side_effects=True, vmem_limit_bytes=8 << 20),
        name="scatter",
    )(
        on_row.reshape((NZL, NY) + tile),
        on_col.reshape((NZH, NX, NK) + tile),
    )
    new_forces = row_share + col_share
    new_velocities = velocities + 0.5 * time_step * (old_forces + new_forces)
    return moved, new_velocities, new_forces


def solution(mesh):
    in_specs = (
        P(None, ("row", "col")),
        P(None, ("row", "col")),
        P(None, ("row", "col")),
        P(("row", "col")),
        P(),
        P(),
        P("row", "col", None, None),
        P("row", "col"),
    )
    out_specs = (P(None, ("row", "col")), P(None, ("row", "col")), P(None, ("row", "col")))
    return jax.shard_map(body, mesh=mesh, in_specs=in_specs, out_specs=out_specs, check_vma=False)
```
